256 devices in a mesh: row: 16 (over z, core), rep: 16 (over x, y).
Axes of the slice: x: 4, y: 4, z: 8, core: 2. Of those that a mesh axis runs over, the one named last changes fastest.
Arguments:
- basis: bfloat16 [32, 524288], P(None, ('row', 'rep')), may hold values from -6 to 6
- precond: float32 [524288], P(('row', 'rep')), may hold values from 0.1 to 0.4
- tiles: bfloat16 [8192, 256, 256], P(('row', 'rep')), as said below
- tile_rows: int32 [8192], P(('row', 'rep')), may hold values from 0 to 127, as said below
- tile_cols: int32 [8192], P(('row', 'rep')), may hold values from 0 to 127, as said below
Outputs:
- directions: float32 [32, 524288], P(None, ('row', 'rep'))
- projected: float32 [64, 64], replicated
The draws below stay inside these ranges and needn't reach their ends.
Inputs may be any that keep to these rules, and one draw needn't show every extreme that they name: The matrix A assembled from all tiles as the steps say is symmetric. `tile_rows`: each device's 32 entries index tile-rows of its band, which are held by the devices of its index along row, in the order of rep. The first 8 entries of a device are its diagonal tiles: the t-th is (index along rep) * 8 + t. Of the other entries none falls in the device's own index along rep, and at most 2 fall in the tile-rows of any one other index along rep, exactly 2 for some. `tile_cols`: each device's 32 entries index tile-columns held by the devices of its index along rep, in the order of row. The first 8 entries of a device are (index along row) * 8 + t for the t-th. Of the other entries none falls in the device's own index along row, and at most 2 fall in the tile-columns of any one other index along row, exactly 2 for some.
All inputs are finite; a program needn't handle non-finite values.
Results may differ from the reference program's by a relative error of at most 0.0003.
Values sent between devices are 32-bit elements; how exact they have to be, the bound alone decides.
A program may use at most 64 MiB of HBM per device.

```python
import math
import jax
import jax.numpy as jnp
from jax import lax

TB = 256
NEIG = 32
TPD = 8
INNER = 1
PAIRS = 12
TILE_DEV = 32
NN = 524288
N_ROW = 16
N_REP = 16


outer_level = 1.3


inner_level = 1.0


def shift_list(count, slots):
    return 1 + ((slots + 1) * (count // 2) - 1) % (count - 1)


def layout(key):
    devices = N_ROW * N_REP
    sources = jnp.arange(devices, dtype=jnp.int32)
    row_of = sources // N_REP
    rep_of = sources % N_REP
    slots = jnp.arange(PAIRS, dtype=jnp.int32)
    row_shift = shift_list(N_ROW, slots)
    rep_shift = shift_list(N_REP, slots)
    target_row = (row_of[None, :] + row_shift[:, None]) % N_ROW
    target_rep = (rep_of[None, :] + rep_shift[:, None]) % N_REP
    source_row = (row_of[None, :] - row_shift[:, None]) % N_ROW
    source_rep = (rep_of[None, :] - rep_shift[:, None]) % N_REP
    inverse = (source_row * N_REP + source_rep).astype(jnp.int32)
    first_offset = jax.random.randint(jax.random.fold_in(key, 102), (PAIRS, devices), 0, TPD, dtype=jnp.int32)
    second_offset = jax.random.randint(jax.random.fold_in(key, 103), (PAIRS, devices), 0, TPD, dtype=jnp.int32)
    own_rows = target_rep * TPD + first_offset
    own_cols = target_row * TPD + second_offset
    back_rows = source_rep * TPD + jnp.take_along_axis(second_offset, inverse, axis=1)
    back_cols = source_row * TPD + jnp.take_along_axis(first_offset, inverse, axis=1)
    steps_local = jnp.arange(TPD, dtype=jnp.int32)[None, :]
    diagonal_rows = rep_of[:, None] * TPD + steps_local
    diagonal_cols = row_of[:, None] * TPD + steps_local
    all_rows = jnp.concatenate([diagonal_rows, own_rows.T, back_rows.T], axis=1).reshape(-1)
    all_cols = jnp.concatenate([diagonal_cols, own_cols.T, back_cols.T], axis=1).reshape(-1)
    return (all_rows.astype(jnp.int32), all_cols.astype(jnp.int32), inverse)


def draw_tile_rows(key, part):
    return layout(key)[0]


def draw_tile_cols(key, part):
    return layout(key)[1]


def draw_tiles(key, part):
    devices = N_ROW * N_REP
    inverse = layout(key)[2]
    slot_index = jnp.arange(PAIRS, dtype=jnp.int32)[:, None]
    slot_order = jax.random.permutation(jax.random.fold_in(key, 107), jnp.arange(PAIRS, dtype=jnp.int32))
    ladder = 0.5 * jnp.power(4.0, slot_order.astype(jnp.float32) / max(PAIRS - 1, 1))
    outer_tiles = jax.random.normal(jax.random.fold_in(key, 104), (PAIRS, devices, TB, TB), jnp.float32) * (outer_level / jnp.sqrt(1.0 * TB))
    outer_tiles = outer_tiles * ladder[:, None, None, None]
    mirrored = jnp.swapaxes(outer_tiles[slot_index, inverse], 2, 3)
    noise = jax.random.normal(jax.random.fold_in(key, 105), (devices, TPD, TB, TB), jnp.float32) * (inner_level / jnp.sqrt(1.0 * TB))
    levels = jax.random.uniform(jax.random.fold_in(key, 106), (devices, TPD, TB), jnp.float32, 3.0, 5.0)
    identity = jnp.eye(TB, dtype=jnp.float32)
    diagonal_tiles = 0.5 * (noise + jnp.swapaxes(noise, 2, 3)) + levels[:, :, :, None] * identity[None, None, :, :]
    whole = jnp.concatenate([diagonal_tiles, jnp.swapaxes(outer_tiles, 0, 1), jnp.swapaxes(mirrored, 0, 1)], axis=1)
    return whole.reshape(-1, TB, TB).astype(jnp.bfloat16)


def block_levels(key, extent, shards, least, top_value):
    def one(dim, blocks):
        steps = jax.random.uniform(jax.random.fold_in(jax.random.fold_in(key, 6), dim), (blocks,), jnp.float32, least / len(shards), top_value / len(shards))
        return jnp.repeat(jnp.exp(steps), extent[dim] // blocks).reshape((-1,) + (1,) * (len(extent) - dim - 1))

    factor_of = one(*shards[0])
    for cut in shards[1:]:
        factor_of = factor_of * one(*cut)
    return factor_of


def bell_draw(own_key, extent, width, bound, split=(), kind=jnp.bfloat16):
    gain = block_levels(own_key, extent, split, -0.22, 0.18) if split else 1.0
    array = jax.random.normal(own_key, extent, jnp.float32) * width * gain
    return jnp.minimum(jnp.maximum(array, -bound), bound).astype(kind)


def setup_inputs(seed: int = 0) -> dict:
    seeds = jax.random.split(jax.random.key(seed), 6)
    basis = bell_draw(seeds[0], (NEIG, NN), 1.0, 6.0, ((1, 256),))
    precond = jnp.clip(jnp.exp(math.log(0.4) - 1.3862944 * jax.random.uniform(seeds[1], (NN,), jnp.float32) ** block_levels(seeds[1], (NN,), ((0, 256),), -0.2, 0.2)), 0.1, 0.4)
    tiles = draw_tiles(jax.random.fold_in(seeds[5], 71), 0)
    tile_rows = draw_tile_rows(jax.random.fold_in(seeds[5], 71), 0)
    tile_cols = draw_tile_cols(jax.random.fold_in(seeds[5], 71), 0)
    return dict(basis=basis, precond=precond, tiles=tiles, tile_rows=tile_rows, tile_cols=tile_cols)


def apply_matrix(vectors, tiles, tile_rows, tile_cols):
    devices = N_ROW * N_REP
    band = N_REP * TPD * TB
    tiles_grouped = tiles.reshape(devices, TILE_DEV, TB, TB)
    rows_grouped = tile_rows.reshape(devices, TILE_DEV)
    cols_grouped = tile_cols.reshape(devices, TILE_DEV)
    offsets = jnp.arange(TB, dtype=jnp.int32)
    bands = jnp.arange(N_REP * TPD, dtype=jnp.int32)

    def accumulate(total, item):
        tile_block, row_local, col_local, device = item
        band_index = device // N_REP
        column_set = device % N_REP
        global_cols = (col_local // TPD * N_REP + column_set) * TPD + col_local % TPD
        positions = (global_cols[:, None] * TB + offsets[None, :]).reshape(-1).astype(jnp.int32)
        picked = jnp.take(vectors, positions, axis=1).reshape(NEIG, TILE_DEV, TB)
        products = jnp.einsum('kjc,jrc->kjr', picked.astype(jnp.float32), tile_block.astype(jnp.float32), precision=lax.Precision.HIGHEST)
        selector = (row_local[:, None] == bands[None, :]).astype(jnp.float32)
        partial_value = jnp.einsum('kjr,jb->kbr', products, selector, precision=lax.Precision.HIGHEST).reshape(NEIG, band)
        begin = (band_index * band).astype(jnp.int32)
        zero_index = jnp.zeros((), jnp.int32)
        current = lax.dynamic_slice(total, (zero_index, begin), (NEIG, band))
        total = lax.dynamic_update_slice(total, current + partial_value, (zero_index, begin))
        return (total, None)
    start_total = jnp.zeros((NEIG, NN), jnp.float32)
    total, unused = lax.scan(accumulate, start_total, (tiles_grouped, rows_grouped, cols_grouped, jnp.arange(devices, dtype=jnp.int32)))
    return total

def reference(basis, precond, tiles, tile_rows, tile_cols):
    highest = lax.Precision.HIGHEST
    basis_float = basis.astype(jnp.float32)

    def project(block):
        coefficients = jnp.dot(block, basis_float.T, precision=highest) / NN
        return block - jnp.dot(coefficients, basis_float, precision=highest)
    applied = apply_matrix(basis_float, tiles, tile_rows, tile_cols)
    ritz_values = jnp.sum(basis_float * applied, axis=1) / NN
    residual = applied - ritz_values[:, None] * basis_float
    correlation = jnp.dot(residual, basis_float.T, precision=highest) / NN
    right_side = -(residual - jnp.dot(correlation, basis_float, precision=highest))
    correction = project(precond[None, :] * right_side)
    for iteration in range(INNER):
        image_block = apply_matrix(correction, tiles, tile_rows, tile_cols)
        updated = correction + precond[None, :] * (right_side - (image_block - ritz_values[:, None] * correction))
        correction = project(updated)
    correction_gram = jnp.dot(correction, correction.T, precision=highest) / NN
    factor = jnp.linalg.cholesky(correction_gram)
    directions = lax.linalg.triangular_solve(factor, correction, left_side=True, lower=True)
    adirections = apply_matrix(directions, tiles, tile_rows, tile_cols)
    block_basis = jnp.dot(basis_float, applied.T, precision=highest) / NN
    block_cross = jnp.dot(basis_float, adirections.T, precision=highest) / NN
    block_new = jnp.dot(directions, adirections.T, precision=highest) / NN
    upper = jnp.concatenate([block_basis, block_cross], axis=1)
    lower = jnp.concatenate([block_cross.T, block_new], axis=1)
    projected = jnp.concatenate([upper, lower], axis=0)
    return (directions, projected)
```

```python
import functools
import jax
import jax.numpy as jnp
from jax import lax
from jax.experimental import pallas as pl
from jax.experimental.pallas import tpu as pltpu
from jax.sharding import PartitionSpec as P

MESH = pl.DeviceIdType.MESH
F32 = jnp.float32
BF16 = jnp.bfloat16
HIGHEST = lax.Precision.HIGHEST


def fetches(me, peer_core, delta, chips):
    same = peer_core == me % 2
    half = chips // 2
    straight = (delta < half) | ((delta == half) & (me // 2 < half))
    return (delta == 0) | (same == straight)


def request_table(tile_rows, tile_cols, each, rows, reps):
    row = lax.axis_index("row")
    rep = lax.axis_index("rep")
    chips = rows // 2
    other_rows = tile_rows[each:]
    other_cols = tile_cols[each:]
    col_peer = other_cols // each
    row_peer = other_rows // each
    delta = lax.rem(col_peer // 2 - row // 2 + chips, chips)
    chosen = fetches(row, col_peer % 2, delta, chips)
    place = jnp.arange(other_rows.shape[0], dtype=jnp.int32)
    earlier = place[None, :] < place[:, None]
    col_rank = jnp.sum(
        (earlier & (col_peer[:, None] == col_peer[None, :])).astype(jnp.int32), axis=1
    )
    row_rank = jnp.sum(
        (earlier & chosen[None, :] & (row_peer[:, None] == row_peer[None, :])).astype(jnp.int32),
        axis=1,
    )
    z_slot = 2 * delta + col_rank
    x_slot = 2 * (lax.rem(row_peer - rep + reps, reps) - 1) + row_rank
    z_code = (each + place) + x_slot * 256 + (other_cols % each) * 65536 + 16777216
    x_code = z_slot + (other_rows % each) * 65536 + 16777216
    z_slot = jnp.where(chosen, z_slot, -1)
    x_slot = jnp.where(chosen, x_slot + 2 * chips, -1)
    slots = jnp.arange(2 * (chips + reps - 1), dtype=jnp.int32)
    slots = jnp.broadcast_to(slots[:, None, None], (slots.shape[0], 128, 1))
    code = jnp.sum(
        jnp.where(slots == z_slot, z_code, 0) + jnp.where(slots == x_slot, x_code, 0), axis=2
    )
    code = jnp.where(code == 0, each * 65536, code)
    return code.reshape(chips + reps - 1, 2, 128)


def split(x):
    high = x.astype(BF16)
    low = (x - high.astype(F32)).astype(BF16)
    return high, low


def stacked(x):
    return jnp.concatenate(split(x), axis=0)


def folded(x):
    half = x.shape[0] // 2
    return x[:half] + x[half:]


def dot(a, b):
    return lax.dot_general(a, b, (((1,), (0,)), ((), ())), preferred_element_type=F32)


def dot_t(a, b):
    return lax.dot_general(a, b, (((1,), (1,)), ((), ())), preferred_element_type=F32)


def exact(a, b):
    return lax.dot_general(
        a, b, (((1,), (0,)), ((), ())), precision=HIGHEST, preferred_element_type=F32
    )


def exact_t(a, b):
    return lax.dot_general(
        a, b, (((1,), (1,)), ((), ())), precision=HIGHEST, preferred_element_type=F32
    )


def inverse_factor(gram):
    n = gram.shape[0]
    row_of = lax.broadcasted_iota(jnp.int32, (n, n), 0)
    col_of = lax.broadcasted_iota(jnp.int32, (n, n), 1)
    work = jnp.concatenate([gram, (row_of == col_of).astype(F32)], axis=1)
    which = lax.broadcasted_iota(jnp.int32, (n, 1), 0)
    for j in range(n):
        scale = lax.rsqrt(work[j : j + 1, j : j + 1])
        pivot = work[j : j + 1, :] * scale
        ratio = work[:, j : j + 1] * scale
        work = jnp.where(
            which == j, pivot, work - jnp.where(which > j, ratio, 0.0) * pivot
        )
    return work[:, n:]


def kernel(
    rows,
    reps,
    scale,
    codes,
    request,
    basis,
    precond,
    tiles_far,
    directions,
    projected,
    tiles,
    wanted,
    wants,
    base,
    weight,
    weight_sz,
    weight_sx,
    weight_rz,
    weight_rx,
    sz1,
    sx1,
    rz1,
    rx1,
    sz2,
    sx2,
    rz2,
    rx2,
    sz3,
    sx3,
    rz3,
    rx3,
    prod_i,
    prod_j1,
    prod_j2,
    tx1,
    tx2,
    bz1,
    bx1,
    bz2,
    bx2,
    diag,
    applied,
    right,
    seed,
    updated,
    m1,
    a1,
    b1,
    c1,
    m2,
    a2,
    b2,
    c2,
    piece,
    gathered,
    m3,
    a3,
    b3,
    small,
    send,
    recv,
    local,
):
    row = lax.axis_index("row")
    rep = lax.axis_index("rep")
    chips = rows // 2
    each = base.shape[0]
    size = base.shape[2]
    count = base.shape[1]
    z_slots = 2 * chips
    x_slots = 2 * (reps - 1)
    chip = row // 2
    core = lax.rem(row, 2)

    diag_load = pltpu.make_async_copy(
        tiles_far.at[pl.ds(0, each)], tiles.at[pl.ds(0, each)], local.at[0]
    )
    rest = tiles.shape[0] - each
    other_load = pltpu.make_async_copy(
        tiles_far.at[pl.ds(each, rest)], tiles.at[pl.ds(each, rest)], local.at[1]
    )
    diag_load.start()
    other_load.start()

    barrier = pltpu.get_barrier_semaphore()
    for d in range(1, rows):
        pl.semaphore_signal(
            barrier, inc=1, device_id={"row": lax.rem(row + d, rows)}, device_id_type=MESH
        )
    for d in range(1, reps):
        pl.semaphore_signal(
            barrier, inc=1, device_id={"rep": lax.rem(rep + d, reps)}, device_id_type=MESH
        )

    def z_holder(delta):
        half = chips // 2
        if delta == 0:
            other = 1 - core
        elif delta < half:
            other = core
        elif delta > half:
            other = 1 - core
        else:
            other = jnp.where(chip < half, core, 1 - core)
        return {"row": lax.rem(chip + delta, chips) * 2 + other}

    def z_reader(delta):
        half = chips // 2
        there = lax.rem(chip - delta + chips, chips)
        if delta == 0:
            other = 1 - core
        elif delta < half:
            other = core
        elif delta > half:
            other = 1 - core
        else:
            other = jnp.where(there < half, core, 1 - core)
        return {"row": there * 2 + other}

    def x_holder(sigma):
        return {"rep": lax.rem(rep + sigma, reps)}

    def x_reader(sigma):
        return {"rep": lax.rem(rep - sigma + reps, reps)}

    def push(source, target, key, device):
        pltpu.make_async_remote_copy(
            src_ref=source,
            dst_ref=target,
            send_sem=send.at[key],
            recv_sem=recv.at[key],
            device_id=device,
            device_id_type=MESH,
        ).start()

    def landed(buffer, key):
        pltpu.make_async_copy(buffer, buffer, recv.at[key]).wait()

    def gone(buffer, key):
        pltpu.make_async_copy(buffer, buffer, send.at[key]).wait()

    for t in range(each):
        base[t] = basis[:, t * size : (t + 1) * size].astype(F32)
        weight[t] = precond[:, t * size : (t + 1) * size]

    pl.semaphore_wait(barrier, rows + reps - 2)

    for delta in range(chips):
        push(request.at[delta], wanted.at[delta], 0, z_holder(delta))
    for sigma in range(1, reps):
        push(request.at[chips + sigma - 1], wanted.at[chips + sigma - 1], 0, x_holder(sigma))

    diag_load.wait()
    for t in range(each):
        diag[t] = dot_t(basis[:, t * size : (t + 1) * size], tiles[t])

    landed(wanted, 0)
    to_scalars = pltpu.make_async_copy(wanted, wants, local.at[2])
    to_scalars.start()
    to_scalars.wait()

    def z_asked(slot):
        return (wants[slot // 2, slot % 2, 0] // 65536) % each

    def x_asked(slot):
        return (wants[chips + slot // 2, slot % 2, 0] // 65536) % each

    def pack(source, to_z, to_x):
        for slot in range(z_slots):
            to_z[slot] = source[z_asked(slot)]
        for slot in range(x_slots):
            to_x[slot] = source[x_asked(slot)]

    def fetch_steps(from_z, from_x, to_z, to_x, key):
        def z_step(delta):
            part = pl.ds(2 * delta, 2)
            return lambda: push(from_z.at[part], to_z.at[part], key, z_reader(delta))

        def x_step(sigma):
            part = pl.ds(2 * (sigma - 1), 2)
            return lambda: push(from_x.at[part], to_x.at[part], key + 1, x_reader(sigma))

        half = chips // 2
        z_order = sorted(range(chips), key=lambda delta: -min(delta, chips - delta))
        z_steps = [z_step(delta) for delta in z_order]
        x_steps = [x_step(sigma) for sigma in range(1, reps)]
        steps = []
        while z_steps or x_steps:
            steps += x_steps[:2] + z_steps[:1]
            x_steps = x_steps[2:]
            z_steps = z_steps[1:]
        return steps

    def z_code(slot):
        return codes[slot // 2, slot % 2, 0]

    def tile_of(slot):
        return tiles[z_code(slot) % 256]

    def x_of(slot):
        return (z_code(slot) // 256) % 256

    def x_source(slot):
        return codes[chips + slot // 2, slot % 2, 0] % 256

    def return_steps(parts_i, parts_j, images, packed, to_z, to_x, key):
        for slot in range(z_slots):
            images[slot] = parts_i(slot)
        for slot in range(x_slots):
            packed[slot] = images[x_source(slot)]
        for sigma in range(1, reps):
            part = pl.ds(2 * (sigma - 1), 2)
            push(packed.at[part], to_x.at[part], key + 1, x_holder(sigma))
        for delta in range(1, chips):
            for slot in (2 * delta, 2 * delta + 1):
                parts_j[1][slot] = parts_j[0](slot)
            part = pl.ds(2 * delta, 2)
            push(parts_j[1].at[part], to_z.at[part], key, z_holder(delta))

    def summed(from_z, from_x, target):
        def strip(index, carry):
            begin = pl.multiple_of(index * 8, 8)
            here = pl.ds(begin, 8)
            totals = [diag[t, here, :] for t in range(each)]
            slots = [(from_z, slot, slot // 2, slot % 2) for slot in range(2, z_slots)]
            slots += [
                (from_x, slot, chips + slot // 2, slot % 2) for slot in range(x_slots)
            ]
            for source, slot, peer, place in slots:
                value = source[slot, here, :]
                asked = wanted[peer, place : place + 1, :] // 65536
                for t in range(each):
                    hit = jnp.broadcast_to(asked % 256 == t, (8, 128))
                    hit = jnp.concatenate([hit] * (size // 128), axis=1)
                    totals[t] = totals[t] + jnp.where(hit, value, 0.0)
            for t in range(each):
                target[t, here, :] = totals[t]
            return carry

        lax.fori_loop(0, count // 8, strip, 0)

    def scatter(full, slots, key):
        for d in range(1, rows):
            to = lax.rem(row + d, rows)
            push(full.at[to], slots.at[row], key, {"row": to})
        pltpu.make_async_copy(full.at[row], slots.at[row], recv.at[key]).start()

    def spread(source, slots, key, axis):
        if axis == "row":
            me, length = row, rows
        else:
            me, length = rep, reps
        for d in range(1, length):
            push(source, slots.at[me], key, {axis: lax.rem(me + d, length)})
        pltpu.make_async_copy(source, slots.at[me], recv.at[key]).start()

    def total(slots):
        value = slots[0]
        for i in range(1, slots.shape[0]):
            value = value + slots[i]
        return value

    def reduce_steps(value, full, slots_a, slots_b, slots_c, key, out, which, fillers):
        part = value.shape[0] // rows
        for i in range(rows):
            full[i] = value[i * part : (i + 1) * part, :]
        scatter(full, slots_a, key)
        fillers[0]()
        landed(slots_a, key)
        piece[which] = total(slots_a)
        spread(piece.at[which], slots_b, key + 1, "rep")
        fillers[1]()
        landed(slots_b, key + 1)
        piece[which + 1] = total(slots_b)
        spread(piece.at[which + 1], slots_c, key + 2, "row")
        fillers[2]()
        landed(slots_c, key + 2)
        for i in range(rows):
            out[i * part : (i + 1) * part, :] = slots_c[i]

    pack(base, sz1, sx1)
    for slot in range(z_slots):
        weight_sz[slot] = weight[z_asked(slot)]
    for slot in range(x_slots):
        weight_sx[slot] = weight[x_asked(slot)]
    for step in fetch_steps(sz1, sx1, rz1, rx1, 1):
        step()
    for step in fetch_steps(weight_sz, weight_sx, weight_rz, weight_rx, 3):
        step()
    other_load.wait()
    landed(rz1, 1)
    landed(rx1, 2)
    return_steps(
        lambda slot: dot_t(rz1[slot].astype(BF16), tile_of(slot)),
        (lambda slot: dot(rx1[x_of(slot)].astype(BF16), tile_of(slot)), prod_j1),
        prod_i,
        tx1,
        bz1,
        bx1,
        5,
    )
    landed(bz1.at[pl.ds(2, z_slots - 2)], 5)
    landed(bx1, 6)
    summed(bz1, bx1, applied)

    pack(applied, sz2, sx2)
    steps = fetch_steps(sz2, sx2, rz2, rx2, 7)
    third = (len(steps) + 3) // 4
    for step in steps[:third]:
        step()
    first = jnp.zeros((3 * count, 3 * count), F32)
    for t in range(each):
        block = base[t]
        basis_part = block.astype(BF16)
        first = first + dot_t(
            jnp.concatenate([*split(applied[t]), basis_part], axis=0),
            jnp.concatenate([basis_part, *split(block * weight[t])], axis=0),
        )
    first = jnp.concatenate([first[:count] + first[count : 2 * count], first[2 * count :]], axis=0)
    first = jnp.concatenate(
        [first[:, :count], first[:, count : 2 * count] + first[:, 2 * count :]], axis=1
    )
    first = jnp.concatenate([first[:count], first[count:]], axis=1)

    def run(some):
        def go():
            for step in some:
                step()

        return go

    reduce_steps(
        first * scale,
        m1,
        a1,
        b1,
        c1,
        12,
        gathered,
        0,
        (run(steps[third : 2 * third]), run(steps[2 * third : 3 * third]), run(steps[3 * third :])),
    )
    basis_applied = gathered[:, :count]
    scaled_applied = gathered[:, count : 2 * count]
    basis_gram = gathered[:, 2 * count : 3 * count]
    scaled_gram = gathered[:, 3 * count :]
    row_of = lax.broadcasted_iota(jnp.int32, (count, count), 0)
    col_of = lax.broadcasted_iota(jnp.int32, (count, count), 1)
    ritz = jnp.sum(jnp.where(row_of == col_of, basis_applied, 0.0), axis=1, keepdims=True)
    correlation = basis_applied - ritz * basis_gram
    mixed = correlation + jnp.where(row_of == col_of, ritz, 0.0)
    coefficients = exact(mixed, scaled_gram) - scaled_applied
    both = stacked(jnp.concatenate([mixed, coefficients], axis=0))

    def rebuilt(block, image, scaling):
        parts = folded(dot(both, block.astype(BF16)))
        remainder = parts[:count] - image
        return scaling * remainder - parts[count:], remainder

    for t in range(each):
        value, remainder = rebuilt(base[t], applied[t], weight[t])
        seed[t] = value
        right[t] = remainder
        diag[t] = folded(dot_t(stacked(value), tiles[t]))

    landed(weight_rz, 3)
    landed(weight_rx, 4)
    landed(rz2, 7)
    landed(rx2, 8)

    def forward(slot):
        value, unused = rebuilt(rz1[slot], rz2[slot], weight_rz[slot])
        return folded(dot_t(stacked(value), tile_of(slot)))

    def backward(slot):
        there = x_of(slot)
        value, unused = rebuilt(rx1[there], rx2[there], weight_rx[there])
        return folded(dot(stacked(value), tile_of(slot)))

    return_steps(forward, (backward, prod_j2), prod_i, tx2, bz2, bx2, 9)
    landed(bz2.at[pl.ds(2, z_slots - 2)], 9)
    landed(bx2, 10)
    summed(bz2, bx2, updated)
    for t in range(each):
        updated[t] = seed[t] + weight[t] * (right[t] - (updated[t] - ritz * seed[t]))

    pack(updated, sz3, sx3)
    steps = fetch_steps(sz3, sx3, rz3, rx3, 18)
    third = (len(steps) + 3) // 4
    for step in steps[:third]:
        step()
    second = jnp.zeros((2 * count, 5 * count), F32)
    for t in range(each):
        parts = split(updated[t])
        second = second + dot_t(
            jnp.concatenate(parts, axis=0),
            jnp.concatenate([*parts, base[t].astype(BF16), *split(applied[t])], axis=0),
        )
    second = folded(second)
    second = jnp.concatenate(
        [
            second[:, :count] + second[:, count : 2 * count],
            second[:, 2 * count : 3 * count],
            second[:, 3 * count : 4 * count] + second[:, 4 * count :],
            jnp.zeros((count, count), F32),
        ],
        axis=1,
    )
    reduce_steps(
        second * scale,
        m2,
        a2,
        b2,
        c2,
        15,
        gathered,
        2,
        (run(steps[third : 2 * third]), run(steps[2 * third : 3 * third]), run(steps[3 * third :])),
    )
    new_gram = gathered[:, :count]
    overlap = gathered[:, count : 2 * count]
    new_applied = gathered[:, 2 * count : 3 * count]
    identity = (row_of == col_of).astype(F32)
    correction_gram = new_gram - exact_t(
        exact(overlap, 2.0 * identity - basis_gram), overlap
    )
    inverse = inverse_factor(correction_gram)
    turned = exact(overlap, basis_applied)
    cross = new_applied - turned
    known = exact_t(new_applied, overlap)
    known = exact_t(turned, overlap) - known - exact_t(overlap, new_applied)
    for t in range(each):
        diag[t] = updated[t] - folded(dot(stacked(overlap), base[t].astype(BF16)))
    form = jnp.zeros((2 * count, 2 * count), F32)
    for t in range(each):
        value = stacked(updated[t])
        form = form + dot_t(value, stacked(folded(dot_t(value, tiles[t]))))

    landed(rz3, 18)
    landed(rx3, 19)
    form = 0.5 * form
    for slot in range(z_slots):
        image = folded(dot_t(stacked(rz3[slot]), tile_of(slot)))
        product = dot_t(stacked(rx3[x_of(slot)]), stacked(image))
        used = z_code(slot) >= 16777216
        share = jnp.where(used, 0.5 if slot < 2 else 1.0, 0.0)
        form = form + share * product
    form = folded(form)
    form = (form[:, :count] + form[:, count:]) * scale
    lines = count // 4
    m3[...] = jnp.concatenate([form[i * lines : (i + 1) * lines] for i in range(4)], axis=1)
    spread(m3, a3, 20, "row")
    for t in range(each):
        directions[:, t * size : (t + 1) * size] = exact(inverse, diag[t])
    landed(a3, 20)
    small[...] = total(a3)
    spread(small, b3, 21, "rep")
    projected[:count, :count] = basis_applied
    projected[count:, :count] = exact(inverse, cross)
    projected[:count, count:] = exact_t(cross.T, inverse)
    landed(b3, 21)
    form = total(b3)
    form = jnp.concatenate([form[:, i * count : (i + 1) * count] for i in range(4)], axis=0)
    inner = form + form.T + known
    projected[count:, count:] = exact_t(exact(inverse, inner), inverse)

    gone(request, 0)
    for key, buffer in (
        (1, sz1),
        (2, sx1),
        (3, weight_sz),
        (4, weight_sx),
        (5, bz1.at[pl.ds(2, z_slots - 2)]),
        (6, tx1),
        (7, sz2),
        (8, sx2),
        (9, bz2.at[pl.ds(2, z_slots - 2)]),
        (10, tx2),
        (18, sz3),
        (19, sx3),
        (12, m1.at[pl.ds(0, rows - 1)]),
        (13, b1.at[pl.ds(0, reps - 1)]),
        (14, c1.at[pl.ds(0, rows - 1)]),
        (15, m2.at[pl.ds(0, rows - 1)]),
        (16, b2.at[pl.ds(0, reps - 1)]),
        (17, c2.at[pl.ds(0, rows - 1)]),
        (20, a3.at[pl.ds(0, rows - 1)]),
        (21, b3.at[pl.ds(0, reps - 1)]),
    ):
        gone(buffer, key)


def shards(basis, precond, tiles, tile_rows, tile_cols):
    count, shard = basis.shape
    size = tiles.shape[1]
    each = shard // size
    rows = lax.axis_size("row")
    reps = lax.axis_size("rep")
    chips = rows // 2
    table = request_table(tile_rows, tile_cols, each, rows, reps)
    z_slots = 2 * chips
    x_slots = 2 * (reps - 1)
    z_block = pltpu.VMEM((z_slots, count, size), F32)
    x_block = pltpu.VMEM((x_slots, count, size), F32)
    own = pltpu.VMEM((each, count, size), F32)
    part = count // rows
    lines = count // 4
    by_row = pltpu.VMEM((rows, part, 4 * count), F32)
    by_rep = pltpu.VMEM((reps, part, 4 * count), F32)
    scratch = [
        pltpu.VMEM(tiles.shape, BF16),
        pltpu.VMEM(table.shape, jnp.int32),
        pltpu.SMEM(table.shape, jnp.int32),
        own,
        pltpu.VMEM((each, 1, size), F32),
        pltpu.VMEM((z_slots, 1, size), F32),
        pltpu.VMEM((x_slots, 1, size), F32),
        pltpu.VMEM((z_slots, 1, size), F32),
        pltpu.VMEM((x_slots, 1, size), F32),
        *([z_block, x_block, z_block, x_block] * 3),
        z_block,
        z_block,
        z_block,
        x_block,
        x_block,
        z_block,
        x_block,
        z_block,
        x_block,
        *([own] * 5),
        by_row,
        by_row,
        by_rep,
        by_row,
        by_row,
        by_row,
        by_rep,
        by_row,
        pltpu.VMEM((4, part, 4 * count), F32),
        pltpu.VMEM((count, 4 * count), F32),
        pltpu.VMEM((lines, 4 * count), F32),
        pltpu.VMEM((rows, lines, 4 * count), F32),
        pltpu.VMEM((reps, lines, 4 * count), F32),
        pltpu.VMEM((lines, 4 * count), F32),
        pltpu.SemaphoreType.DMA((22,)),
        pltpu.SemaphoreType.DMA((22,)),
        pltpu.SemaphoreType.DMA((3,)),
    ]
    vmem = pl.BlockSpec(memory_space=pltpu.VMEM)
    return pl.pallas_call(
        functools.partial(kernel, rows, reps, 1.0 / (shard * rows * reps)),
        name="davidson_step",
        out_shape=(
            jax.ShapeDtypeStruct((count, shard), F32),
            jax.ShapeDtypeStruct((2 * count, 2 * count), F32),
        ),
        in_specs=[
            pl.BlockSpec(memory_space=pltpu.SMEM),
            vmem,
            vmem,
            vmem,
            pl.BlockSpec(memory_space=pl.ANY),
        ],
        out_specs=(vmem, vmem),
        scratch_shapes=scratch,
        compiler_params=pltpu.CompilerParams(
            collective_id=0, has_side_effects=True, vmem_limit_bytes=56 * 1024 * 1024
        ),
    )(table, table, basis, precond.reshape(1, shard), tiles)


def solution(mesh):
    both = ("row", "rep")
    placed = (P(None, both), P(both), P(both, None, None), P(both), P(both))
    return jax.shard_map(
        shards, mesh=mesh, in_specs=placed, out_specs=(P(None, both), P()), check_vma=False
    )
```

```python
import functools
import math
import jax
import jax.numpy as jnp
from jax import lax
from jax.experimental import pallas as pl
from jax.experimental.pallas import tpu as pltpu
from jax.sharding import PartitionSpec as P

MESH = pl.DeviceIdType.MESH
F32 = jnp.float32
BF16 = jnp.bfloat16
HIGHEST = lax.Precision.HIGHEST


def fetches(me, peer_core, delta, chips):
    same = peer_core == me % 2
    half = chips // 2
    straight = (delta < half) | ((delta == half) & (me // 2 < half))
    return (delta == 0) | (same == straight)


def request_table(tile_rows, tile_cols, each, rows, reps):
    row = lax.axis_index("row")
    rep = lax.axis_index("rep")
    chips = rows // 2
    other_rows = tile_rows[each:]
    other_cols = tile_cols[each:]
    col_peer = other_cols // each
    row_peer = other_rows // each
    delta = lax.rem(col_peer // 2 - row // 2 + chips, chips)
    chosen = fetches(row, col_peer % 2, delta, chips)
    place = jnp.arange(other_rows.shape[0], dtype=jnp.int32)
    earlier = place[None, :] < place[:, None]
    col_rank = jnp.sum(
        (earlier & (col_peer[:, None] == col_peer[None, :])).astype(jnp.int32), axis=1
    )
    row_rank = jnp.sum(
        (earlier & chosen[None, :] & (row_peer[:, None] == row_peer[None, :])).astype(jnp.int32),
        axis=1,
    )
    z_slot = 2 * delta + col_rank
    side = math.isqrt(reps)
    shift = lax.rem(row_peer // side - rep // side + side, side) * side
    shift = shift + lax.rem(row_peer % side - rep % side + side, side)
    x_slot = 2 * (shift - 1) + row_rank
    z_code = (each + place) + x_slot * 256 + (other_cols % each) * 65536 + 16777216
    x_code = z_slot + (other_rows % each) * 65536 + 16777216
    z_slot = jnp.where(chosen, z_slot, -1)
    x_slot = jnp.where(chosen, x_slot + 2 * chips, -1)
    slots = jnp.arange(2 * (chips + reps - 1), dtype=jnp.int32)
    slots = jnp.broadcast_to(slots[:, None, None], (slots.shape[0], 128, 1))
    code = jnp.sum(
        jnp.where(slots == z_slot, z_code, 0) + jnp.where(slots == x_slot, x_code, 0), axis=2
    )
    code = jnp.where(code == 0, each * 65536, code)
    return code.reshape(chips + reps - 1, 2, 128)


def split(x):
    high = x.astype(BF16)
    low = (x - high.astype(F32)).astype(BF16)
    return high, low


def stacked(x):
    return jnp.concatenate(split(x), axis=0)


def folded(x):
    half = x.shape[0] // 2
    return x[:half] + x[half:]


def dot(a, b):
    return lax.dot_general(a, b, (((1,), (0,)), ((), ())), preferred_element_type=F32)


def dot_t(a, b):
    return lax.dot_general(a, b, (((1,), (1,)), ((), ())), preferred_element_type=F32)


def exact(a, b):
    return lax.dot_general(
        a, b, (((1,), (0,)), ((), ())), precision=HIGHEST, preferred_element_type=F32
    )


def exact_t(a, b):
    return lax.dot_general(
        a, b, (((1,), (1,)), ((), ())), precision=HIGHEST, preferred_element_type=F32
    )


def eliminated(work, begin, end):
    which = lax.broadcasted_iota(jnp.int32, (work.shape[0], 1), 0)
    for j in range(begin, end):
        scale = lax.rsqrt(work[j : j + 1, j : j + 1])
        pivot = work[j : j + 1, :] * scale
        ratio = work[:, j : j + 1] * scale
        work = jnp.where(
            which == j, pivot, work - jnp.where(which > j, ratio, 0.0) * pivot
        )
    return work


KEYS = {}
for name in ("request", "weight_z", "weight_x", "low_a", "low_b", "low_c", "mid_a", "mid_b"):
    KEYS[name] = len(KEYS)
for name in ("new_a", "new_b", "new_c", "end_a", "end_b"):
    KEYS[name] = len(KEYS)
for half in range(2):
    for name in ("z1", "x1", "bz1", "bx1", "z2", "x2", "bz2", "bx2", "z3", "x3"):
        KEYS[name, half] = len(KEYS)


def kernel(
    rows,
    reps,
    halves,
    scale,
    codes,
    request,
    basis,
    precond,
    tiles_far,
    directions,
    projected,
    tiles,
    wanted,
    wants,
    base,
    weight,
    weight_sz,
    weight_sx,
    weight_rz,
    weight_rx,
    sz1,
    sx1,
    rz1,
    rx1a,
    rx1b,
    sz2,
    sx2,
    rz2,
    rx2a,
    rx2b,
    sz3,
    sx3,
    rz3,
    rx3a,
    rx3b,
    prod_i1,
    prod_i2,
    prod_j1,
    prod_j2,
    tx1,
    tx2,
    bz1,
    bx1,
    bz2,
    bx2,
    diag,
    applied,
    right,
    seed,
    updated,
    low_m,
    low_a,
    low_b,
    low_c,
    low_piece,
    low,
    mid_m,
    mid_a,
    mid_n,
    mid_b,
    new_m,
    new_a,
    new_b,
    new_c,
    new_piece,
    new,
    end_m,
    end_a,
    end_n,
    end_b,
    send,
    recv,
    local,
):
    rx1, rx2, rx3 = (rx1a, rx1b), (rx2a, rx2b), (rx3a, rx3b)
    row = lax.axis_index("row")
    rep = lax.axis_index("rep")
    chips = rows // 2
    each = base.shape[0]
    size = base.shape[2]
    count = base.shape[1]
    z_slots = 2 * chips
    x_slots = 2 * (reps - 1)
    side = math.isqrt(reps)
    chip = row // 2
    core = lax.rem(row, 2)
    part = count // halves

    diag_load = pltpu.make_async_copy(
        tiles_far.at[pl.ds(0, each)], tiles.at[pl.ds(0, each)], local.at[0]
    )
    rest = tiles.shape[0] - each
    other_load = pltpu.make_async_copy(
        tiles_far.at[pl.ds(each, rest)], tiles.at[pl.ds(each, rest)], local.at[1]
    )
    diag_load.start()
    other_load.start()

    barrier = pltpu.get_barrier_semaphore()
    for d in range(1, rows):
        pl.semaphore_signal(
            barrier, inc=1, device_id={"row": lax.rem(row + d, rows)}, device_id_type=MESH
        )
    for d in range(1, reps):
        pl.semaphore_signal(
            barrier, inc=1, device_id={"rep": lax.rem(rep + d, reps)}, device_id_type=MESH
        )

    def z_holder(delta):
        half = chips // 2
        if delta == 0:
            other = 1 - core
        elif delta < half:
            other = core
        elif delta > half:
            other = 1 - core
        else:
            other = jnp.where(chip < half, core, 1 - core)
        return {"row": lax.rem(chip + delta, chips) * 2 + other}

    def z_reader(delta):
        half = chips // 2
        there = lax.rem(chip - delta + chips, chips)
        if delta == 0:
            other = 1 - core
        elif delta < half:
            other = core
        elif delta > half:
            other = 1 - core
        else:
            other = jnp.where(there < half, core, 1 - core)
        return {"row": there * 2 + other}

    def x_holder(sigma):
        across = lax.rem(rep // side + sigma // side, side)
        along = lax.rem(lax.rem(rep, side) + sigma % side, side)
        return {"rep": across * side + along}

    def x_reader(sigma):
        across = lax.rem(rep // side - sigma // side + side, side)
        along = lax.rem(lax.rem(rep, side) - sigma % side + side, side)
        return {"rep": across * side + along}

    def push(source, target, key, device):
        pltpu.make_async_remote_copy(
            src_ref=source,
            dst_ref=target,
            send_sem=send.at[KEYS[key]],
            recv_sem=recv.at[KEYS[key]],
            device_id=device,
            device_id_type=MESH,
        ).start()

    def landed(buffer, key):
        pltpu.make_async_copy(buffer, buffer, recv.at[KEYS[key]]).wait()

    def gone(buffer, key):
        pltpu.make_async_copy(buffer, buffer, send.at[KEYS[key]]).wait()

    def scatter(full, slots, key):
        for d in range(1, rows):
            to = lax.rem(row + d, rows)
            push(full.at[to], slots.at[row], key, {"row": to})
        pltpu.make_async_copy(full.at[row], slots.at[row], recv.at[KEYS[key]]).start()

    def spread(source, slots, key, axis):
        if axis == "row":
            me, length = row, rows
        else:
            me, length = rep, reps
        for d in range(1, length):
            push(source, slots.at[me], key, {axis: lax.rem(me + d, length)})
        pltpu.make_async_copy(source, slots.at[me], recv.at[KEYS[key]]).start()

    def total(slots):
        value = slots[0]
        for i in range(1, slots.shape[0]):
            value = value + slots[i]
        return value

    def cut(value, full):
        lines = full.shape[1]
        for i in range(full.shape[0]):
            full[i] = value[i * lines : (i + 1) * lines, :]

    def joined(slots, whole):
        lines = slots.shape[1]
        for i in range(slots.shape[0]):
            whole[i * lines : (i + 1) * lines, :] = slots[i]

    def scaled(block, scaling):
        return jnp.concatenate([block.astype(BF16), *split(block * scaling)], axis=0)

    own_low = jnp.zeros((count, 3 * count), F32)
    for t in range(each):
        block = basis[:, t * size : (t + 1) * size]
        base[t] = block.astype(F32)
        weight[t] = precond[:, t * size : (t + 1) * size]
        own_low = own_low + dot_t(block, scaled(base[t], weight[t]))
    own_low = own_low * scale
    own_low = jnp.concatenate(
        [own_low[:, :count], own_low[:, count : 2 * count] + own_low[:, 2 * count :]], axis=1
    )
    cut(jnp.concatenate([own_low[: count // 2], own_low[count // 2 :]], axis=1), low_m)

    pl.semaphore_wait(barrier, rows + reps - 2)

    for delta in range(chips):
        push(request.at[delta], wanted.at[delta], "request", z_holder(delta))
    for sigma in range(1, reps):
        here = chips + sigma - 1
        push(request.at[here], wanted.at[here], "request", x_holder(sigma))
    scatter(low_m, low_a, "low_a")

    diag_load.wait()
    for t in range(each):
        diag[t] = dot_t(basis[:, t * size : (t + 1) * size], tiles[t])

    landed(wanted, "request")
    to_scalars = pltpu.make_async_copy(wanted, wants, local.at[2])
    to_scalars.start()
    to_scalars.wait()
    landed(low_a, "low_a")
    low_piece[0] = total(low_a)
    spread(low_piece.at[0], low_b, "low_b", "rep")

    def rows_of(half):
        return slice(half * part, (half + 1) * part)

    def z_asked(slot):
        return (wants[slot // 2, slot % 2, 0] // 65536) % each

    def x_asked(slot):
        return (wants[chips + slot // 2, slot % 2, 0] // 65536) % each

    def far(size_of, index):
        return -min(index, size_of - index)

    z_order = sorted(range(chips), key=lambda delta: far(chips, delta))
    x_order = sorted(
        range(1, reps), key=lambda sigma: far(side, sigma // side) + far(side, sigma % side)
    )

    def answer(own, to_z, to_x, from_z, from_x, turn, half):
        here = rows_of(half)
        for slot in range(z_slots):
            from_z[half, slot] = own[z_asked(slot), here, :]
        for slot in range(x_slots):
            from_x[half, slot] = own[x_asked(slot), here, :]
        z_left, x_left = list(z_order), list(x_order)
        while z_left or x_left:
            for sigma in x_left[:2]:
                block = pl.ds(2 * (sigma - 1), 2)
                push(
                    from_x.at[half, block], to_x[half].at[block], ("x" + turn, half), x_reader(sigma)
                )
            for delta in z_left[:1]:
                block = pl.ds(2 * delta, 2)
                push(
                    from_z.at[half, block], to_z.at[half, block], ("z" + turn, half), z_reader(delta)
                )
            z_left, x_left = z_left[1:], x_left[2:]

    def z_code(slot):
        return codes[slot // 2, slot % 2, 0]

    def tile_of(slot):
        return tiles[z_code(slot) % 256]

    def x_of(slot):
        return (z_code(slot) // 256) % 256

    def x_source(slot):
        return codes[chips + slot // 2, slot % 2, 0] % 256

    def returned(forward, backward, images, mirrored, packed, to_z, to_x, turn, half):
        for slot in range(z_slots):
            images[half, slot] = forward(slot)
        for slot in range(x_slots):
            packed[half, slot] = images[half, x_source(slot)]
        for sigma in x_order:
            block = pl.ds(2 * (sigma - 1), 2)
            push(
                packed.at[half, block], to_x.at[half, block], ("bx" + turn, half), x_holder(sigma)
            )
        for delta in z_order[:-1]:
            for slot in (2 * delta, 2 * delta + 1):
                mirrored[half, slot] = backward(slot)
            block = pl.ds(2 * delta, 2)
            push(
                mirrored.at[half, block], to_z.at[half, block], ("bz" + turn, half), z_holder(delta)
            )

    inner = pl.ds(2, z_slots - 2)

    def summed(from_z, from_x, target, half):
        def strip(index, carry):
            here = pl.ds(pl.multiple_of(index * 8, 8), 8)
            there = pl.ds(pl.multiple_of(half * part + index * 8, 8), 8)
            totals = [diag[t, there, :] for t in range(each)]
            slots = [(from_z, slot, slot // 2, slot % 2) for slot in range(2, z_slots)]
            slots += [(from_x, slot, chips + slot // 2, slot % 2) for slot in range(x_slots)]
            for source, slot, peer, place in slots:
                value = source[half, slot, here, :]
                asked = wanted[peer, place : place + 1, :] // 65536
                for t in range(each):
                    hit = jnp.broadcast_to(asked % 256 == t, (8, 128))
                    hit = jnp.concatenate([hit] * (size // 128), axis=1)
                    totals[t] = totals[t] + jnp.where(hit, value, 0.0)
            for t in range(each):
                target[t, there, :] = totals[t]
            return carry

        lax.fori_loop(0, part // 8, strip, 0)

    def all_rows(buffer, slot):
        return jnp.concatenate([buffer[half, slot] for half in range(halves)], axis=0)

    def rows_held(buffers, slot):
        return jnp.concatenate([buffer[slot] for buffer in buffers], axis=0)

    for half in range(halves):
        answer(base, rz1, rx1, sz1, sx1, "1", half)
    for slot in range(z_slots):
        weight_sz[slot] = weight[z_asked(slot)]
    for slot in range(x_slots):
        weight_sx[slot] = weight[x_asked(slot)]
    for delta in range(chips):
        block = pl.ds(2 * delta, 2)
        push(weight_sz.at[block], weight_rz.at[block], "weight_z", z_reader(delta))
    for sigma in range(1, reps):
        block = pl.ds(2 * (sigma - 1), 2)
        push(weight_sx.at[block], weight_rx.at[block], "weight_x", x_reader(sigma))
    own_mid = jnp.zeros((2 * count, 3 * count), F32)
    for t in range(each):
        own_mid = own_mid + dot_t(stacked(diag[t]), scaled(base[t], weight[t]))
    other_load.wait()
    for half in range(halves):
        landed(rz1.at[half], ("z1", half))
        landed(rx1[half], ("x1", half))
        if half == 0:
            landed(low_b, "low_b")
            low_piece[1] = total(low_b)
            spread(low_piece.at[1], low_c, "low_c", "row")
        returned(
            lambda slot: dot_t(rz1[half, slot].astype(BF16), tile_of(slot)),
            lambda slot: dot(rx1[half][x_of(slot)].astype(BF16), tile_of(slot)),
            prod_i1,
            prod_j1,
            tx1,
            bz1,
            bx1,
            "1",
            half,
        )
    landed(low_c, "low_c")
    joined(low_c, low)
    landed(weight_rz, "weight_z")
    landed(weight_rx, "weight_x")

    def used(slot):
        return z_code(slot) >= 16777216

    own_form = own_mid[:, :count]
    both_form = jnp.zeros((2 * count, count), F32)
    scaled_form = own_mid[:, count : 2 * count] + own_mid[:, 2 * count :]
    for slot in range(z_slots):
        there = x_of(slot)
        product = dot_t(
            stacked(all_rows(prod_i1, slot)), scaled(rows_held(rx1, there), weight_rx[there])
        )
        product = jnp.where(used(slot), product, 0.0)
        if slot < 2:
            own_form = own_form + product[:, :count]
        else:
            both_form = both_form + product[:, :count]
        scaled_form = scaled_form + product[:, count : 2 * count] + product[:, 2 * count :]
        if slot >= 2:
            product = dot_t(
                stacked(all_rows(prod_j1, slot)),
                stacked(all_rows(rz1, slot) * weight_rz[slot]),
            )
            product = jnp.where(used(slot), product, 0.0)
            scaled_form = scaled_form + product[:, :count] + product[:, count:]
    both_form = folded(both_form + 0.5 * own_form)
    scaled_form = folded(scaled_form)
    quarter = jnp.concatenate([both_form, scaled_form], axis=1) * scale
    mid_m[...] = jnp.concatenate([quarter[: count // 2], quarter[count // 2 :]], axis=1)
    spread(mid_m, mid_a, "mid_a", "rep")

    for half in range(halves):
        landed(bz1.at[half, inner], ("bz1", half))
        landed(bx1.at[half], ("bx1", half))
        summed(bz1, bx1, applied, half)
        if half == halves - 1:
            landed(mid_a, "mid_a")
            mid_n[...] = total(mid_a)
            spread(mid_n, mid_b, "mid_b", "row")
        answer(applied, rz2, rx2, sz2, sx2, "2", half)
    landed(mid_b, "mid_b")
    quarter = total(mid_b)
    quarter = jnp.concatenate([quarter[:, : 2 * count], quarter[:, 2 * count :]], axis=0)
    basis_applied = quarter[:, :count] + quarter[:, :count].T
    scaled_applied = quarter[:, count:]
    basis_gram = jnp.concatenate([low[:, :count], low[:, 2 * count : 3 * count]], axis=0)
    scaled_gram = jnp.concatenate([low[:, count : 2 * count], low[:, 3 * count :]], axis=0)
    row_of = lax.broadcasted_iota(jnp.int32, (count, count), 0)
    col_of = lax.broadcasted_iota(jnp.int32, (count, count), 1)
    ritz = jnp.sum(jnp.where(row_of == col_of, basis_applied, 0.0), axis=1, keepdims=True)
    correlation = basis_applied - ritz * basis_gram
    mixed = correlation + jnp.where(row_of == col_of, ritz, 0.0)
    coefficients = exact(mixed, scaled_gram) - scaled_applied

    for half in range(halves):
        here = rows_of(half)
        both = stacked(jnp.concatenate([mixed[here], coefficients[here]], axis=0))

        def rebuilt(block, image, scaling):
            parts = folded(dot(both, block.astype(BF16)))
            remainder = parts[:part] - image
            return scaling * remainder - parts[part:], remainder

        def forward(slot):
            value, unused = rebuilt(all_rows(rz1, slot), rz2[half, slot], weight_rz[slot])
            return folded(dot_t(stacked(value), tile_of(slot)))

        def backward(slot):
            there = x_of(slot)
            value, unused = rebuilt(rows_held(rx1, there), rx2[half][there], weight_rx[there])
            return folded(dot(stacked(value), tile_of(slot)))

        landed(rz2.at[half], ("z2", half))
        landed(rx2[half], ("x2", half))
        returned(forward, backward, prod_i2, prod_j2, tx2, bz2, bx2, "2", half)
        for t in range(each):
            value, remainder = rebuilt(base[t], applied[t, here, :], weight[t])
            seed[t, here, :] = value
            right[t, here, :] = remainder
            diag[t, here, :] = folded(dot_t(stacked(value), tiles[t]))

    for half in range(halves):
        here = rows_of(half)
        landed(bz2.at[half, inner], ("bz2", half))
        landed(bx2.at[half], ("bx2", half))
        summed(bz2, bx2, updated, half)
        for t in range(each):
            value = seed[t, here, :]
            updated[t, here, :] = value + weight[t] * (
                right[t, here, :] - (updated[t, here, :] - ritz[here] * value)
            )
        if half == halves - 1:
            second = jnp.zeros((2 * count, 5 * count), F32)
            for t in range(each):
                parts = split(updated[t])
                second = second + dot_t(
                    jnp.concatenate(parts, axis=0),
                    jnp.concatenate([*parts, base[t].astype(BF16), *split(applied[t])], axis=0),
                )
            second = folded(second) * scale
            second = jnp.concatenate(
                [
                    second[:, :count] + second[:, count : 2 * count],
                    second[:, 2 * count : 3 * count],
                    second[:, 3 * count : 4 * count] + second[:, 4 * count :],
                    jnp.zeros((count, count), F32),
                ],
                axis=1,
            )
            cut(second, new_m)
            scatter(new_m, new_a, "new_a")
        answer(updated, rz3, rx3, sz3, sx3, "3", half)
    form = jnp.zeros((2 * count, 2 * count), F32)
    for t in range(each):
        value = stacked(updated[t])
        form = form + dot_t(value, stacked(folded(dot_t(value, tiles[t]))))
    form = 0.5 * form
    landed(new_a, "new_a")
    new_piece[0] = total(new_a)
    spread(new_piece.at[0], new_b, "new_b", "rep")
    for half in range(halves):
        landed(rz3.at[half], ("z3", half))
        landed(rx3[half], ("x3", half))
        if half == halves - 1:
            landed(new_b, "new_b")
            new_piece[1] = total(new_b)
            spread(new_piece.at[1], new_c, "new_c", "row")
        for slot in range(z_slots):
            prod_i2[half, slot] = folded(dot_t(stacked(rz3[half, slot]), tile_of(slot)))
    for slot in range(z_slots):
        product = dot_t(stacked(rows_held(rx3, x_of(slot))), stacked(all_rows(prod_i2, slot)))
        form = form + jnp.where(used(slot), 0.5 if slot < 2 else 1.0, 0.0) * product
    form = folded(form)
    form = (form[:, :count] + form[:, count:]) * scale
    lines = count // 4
    end_m[...] = jnp.concatenate([form[i * lines : (i + 1) * lines] for i in range(4)], axis=1)
    spread(end_m, end_a, "end_a", "row")

    landed(new_c, "new_c")
    joined(new_c, new)
    new_gram = new[:, :count]
    overlap = new[:, count : 2 * count]
    new_applied = new[:, 2 * count : 3 * count]
    identity = (row_of == col_of).astype(F32)
    correction_gram = new_gram - exact_t(exact(overlap, 2.0 * identity - basis_gram), overlap)
    work = eliminated(jnp.concatenate([correction_gram, identity], axis=1), 0, count // 2)
    landed(end_a, "end_a")
    end_n[...] = total(end_a)
    spread(end_n, end_b, "end_b", "rep")
    inverse = eliminated(work, count // 2, count)[:, count:]
    turned = exact(overlap, basis_applied)
    cross = new_applied - turned
    known = exact_t(new_applied, overlap)
    known = exact_t(turned, overlap) - known - exact_t(overlap, new_applied)
    projected[:count, :count] = basis_applied
    projected[count:, :count] = exact(inverse, cross)
    projected[:count, count:] = exact_t(cross.T, inverse)
    for t in range(each):
        value = updated[t] - folded(dot(stacked(overlap), base[t].astype(BF16)))
        directions[:, t * size : (t + 1) * size] = exact(inverse, value)
    landed(end_b, "end_b")
    form = total(end_b)
    form = jnp.concatenate([form[:, i * count : (i + 1) * count] for i in range(4)], axis=0)
    middle = form + form.T + known
    projected[count:, count:] = exact_t(exact(inverse, middle), inverse)

    gone(request, "request")
    gone(weight_sz, "weight_z")
    gone(weight_sx, "weight_x")
    for half in range(halves):
        for turn, from_z, from_x in (("1", sz1, sx1), ("2", sz2, sx2), ("3", sz3, sx3)):
            gone(from_z.at[half], ("z" + turn, half))
            gone(from_x.at[half], ("x" + turn, half))
        for turn, from_z, from_x in (("1", prod_j1, tx1), ("2", prod_j2, tx2)):
            gone(from_z.at[half, inner], ("bz" + turn, half))
            gone(from_x.at[half], ("bx" + turn, half))
    other_rows = pl.ds(0, rows - 1)
    other_reps = pl.ds(0, reps - 1)
    for key, buffer in (
        ("low_a", low_a.at[other_rows]),
        ("low_b", low_b.at[other_reps]),
        ("low_c", low_c.at[other_rows]),
        ("mid_a", mid_a.at[other_reps]),
        ("mid_b", mid_b.at[other_rows]),
        ("new_a", new_a.at[other_rows]),
        ("new_b", new_b.at[other_reps]),
        ("new_c", new_c.at[other_rows]),
        ("end_a", end_a.at[other_rows]),
        ("end_b", end_b.at[other_reps]),
    ):
        gone(buffer, key)


def shards(basis, precond, tiles, tile_rows, tile_cols):
    count, shard = basis.shape
    size = tiles.shape[1]
    each = shard // size
    rows = lax.axis_size("row")
    reps = lax.axis_size("rep")
    chips = rows // 2
    halves = 2
    table = request_table(tile_rows, tile_cols, each, rows, reps)
    z_slots = 2 * chips
    x_slots = 2 * (reps - 1)

    def held(*shape):
        return pltpu.VMEM(shape, F32)

    z_block = held(halves, z_slots, count // halves, size)
    x_block = held(halves, x_slots, count // halves, size)
    x_half = held(x_slots, count // halves, size)
    own = held(each, count, size)
    wide = 4 * count
    lines = count // rows
    scratch = [
        pltpu.VMEM(tiles.shape, BF16),
        pltpu.VMEM(table.shape, jnp.int32),
        pltpu.SMEM(table.shape, jnp.int32),
        own,
        held(each, 1, size),
        held(z_slots, 1, size),
        held(x_slots, 1, size),
        held(z_slots, 1, size),
        held(x_slots, 1, size),
        *([z_block, x_block, z_block, *([x_half] * halves)] * 3),
        z_block,
        z_block,
        z_block,
        z_block,
        x_block,
        x_block,
        z_block,
        x_block,
        z_block,
        x_block,
        *([own] * 5),
        held(rows, lines // 2, wide),
        held(rows, lines // 2, wide),
        held(reps, lines // 2, wide),
        held(rows, lines // 2, wide),
        held(2, lines // 2, wide),
        held(count // 2, wide),
        held(count // 2, wide),
        held(reps, count // 2, wide),
        held(count // 2, wide),
        held(rows, count // 2, wide),
        held(rows, lines, wide),
        held(rows, lines, wide),
        held(reps, lines, wide),
        held(rows, lines, wide),
        held(2, lines, wide),
        held(count, wide),
        held(count // 4, wide),
        held(rows, count // 4, wide),
        held(count // 4, wide),
        held(reps, count // 4, wide),
        pltpu.SemaphoreType.DMA((len(KEYS),)),
        pltpu.SemaphoreType.DMA((len(KEYS),)),
        pltpu.SemaphoreType.DMA((3,)),
    ]
    vmem = pl.BlockSpec(memory_space=pltpu.VMEM)
    return pl.pallas_call(
        functools.partial(kernel, rows, reps, halves, 1.0 / (shard * rows * reps)),
        name="davidson_step",
        out_shape=(
            jax.ShapeDtypeStruct((count, shard), F32),
            jax.ShapeDtypeStruct((2 * count, 2 * count), F32),
        ),
        in_specs=[
            pl.BlockSpec(memory_space=pltpu.SMEM),
            vmem,
            vmem,
            vmem,
            pl.BlockSpec(memory_space=pl.ANY),
        ],
        out_specs=(vmem, vmem),
        scratch_shapes=scratch,
        compiler_params=pltpu.CompilerParams(
            collective_id=0, has_side_effects=True, vmem_limit_bytes=56 * 1024 * 1024
        ),
    )(table, table, basis, precond.reshape(1, shard), tiles)


def solution(mesh):
    both = ("row", "rep")
    placed = (P(None, both), P(both), P(both, None, None), P(both), P(both))
    return jax.shard_map(
        shards, mesh=mesh, in_specs=placed, out_specs=(P(None, both), P()), check_vma=False
    )
```

```python
import functools
import math
import jax
import jax.numpy as jnp
from jax import lax
from jax.experimental import pallas as pl
from jax.experimental.pallas import tpu as pltpu
from jax.sharding import PartitionSpec as P

MESH = pl.DeviceIdType.MESH
F32 = jnp.float32
BF16 = jnp.bfloat16
HIGHEST = lax.Precision.HIGHEST


def request_table(tile_rows, tile_cols, row, rep, each, rows, reps):
    entries = tile_rows.shape[1]
    chips = rows // 2
    side = math.isqrt(reps)
    bits = each.bit_length() - 1
    side_bits = side.bit_length() - 1
    place = lax.broadcasted_iota(jnp.int32, (1, entries), 1)
    col_peer = lax.shift_right_logical(tile_cols, bits)
    row_peer = lax.shift_right_logical(tile_rows, bits)
    delta = (lax.shift_right_logical(col_peer, 1) - row // 2 + chips) & (chips - 1)
    limit = chips // 2 + jnp.where(row // 2 < chips // 2, 1, 0)
    differs = (col_peer & 1) ^ lax.rem(row, 2)
    crossed = jnp.where(delta < limit, 0, 1)
    chosen = ((delta == 0) | (differs == crossed)) & (place >= each)
    col_key = jnp.where(chosen, col_peer, -1)
    row_key = jnp.where(chosen, row_peer, -1)
    first = lax.broadcasted_iota(jnp.int32, (entries, entries), 0)
    second = lax.broadcasted_iota(jnp.int32, (entries, entries), 1)

    def rank(key):
        upright = jnp.sum(jnp.where(first == second, key, 0), axis=1, keepdims=True)
        return jnp.sum(
            jnp.where((first < second) & (upright == key), 1, 0), axis=0, keepdims=True
        )

    across = (lax.shift_right_logical(row_peer, side_bits) - rep // side + side) & (side - 1)
    along = ((row_peer & (side - 1)) - lax.rem(rep, side) + side) & (side - 1)
    z_slot = 2 * delta + rank(col_key)
    x_slot = 2 * (across * side + along - 1) + rank(row_key)
    z_code = place + x_slot * 256 + (tile_cols & (each - 1)) * 65536 + 16777216
    x_code = z_slot + (tile_rows & (each - 1)) * 65536 + 16777216
    z_slot = jnp.where(chosen, z_slot, -1)
    x_slot = jnp.where(chosen, x_slot + 2 * chips, -1)
    slots = lax.broadcasted_iota(jnp.int32, (2 * (chips + reps), entries), 0)
    code = jnp.where(slots == z_slot, z_code, 0) + jnp.where(slots == x_slot, x_code, 0)
    code = jnp.sum(code, axis=1, keepdims=True)
    return jnp.broadcast_to(jnp.where(code == 0, each * 65536, code), (code.shape[0], 128))


def split(x):
    high = x.astype(BF16)
    low = (x - high.astype(F32)).astype(BF16)
    return high, low


def stacked(x):
    return jnp.concatenate(split(x), axis=0)


def folded(x):
    half = x.shape[0] // 2
    return x[:half] + x[half:]


def dot(a, b):
    return lax.dot_general(a, b, (((1,), (0,)), ((), ())), preferred_element_type=F32)


def dot_t(a, b):
    return lax.dot_general(a, b, (((1,), (1,)), ((), ())), preferred_element_type=F32)


def exact(a, b):
    return lax.dot_general(
        a, b, (((1,), (0,)), ((), ())), precision=HIGHEST, preferred_element_type=F32
    )


def exact_t(a, b):
    return lax.dot_general(
        a, b, (((1,), (1,)), ((), ())), precision=HIGHEST, preferred_element_type=F32
    )


def eliminated(work, begin, end):
    which = lax.broadcasted_iota(jnp.int32, (work.shape[0], 1), 0)
    for j in range(begin, end):
        scale = lax.rsqrt(work[j : j + 1, j : j + 1])
        pivot = work[j : j + 1, :] * scale
        ratio = work[:, j : j + 1] * scale
        work = jnp.where(
            which == j, pivot, work - jnp.where(which > j, ratio, 0.0) * pivot
        )
    return work


KEYS = {}
for name in ("request", "weight_z", "weight_x", "low_a", "low_b", "low_c", "mid_a", "mid_b"):
    KEYS[name] = len(KEYS)
for name in ("new_a", "new_b", "new_c", "end_a", "end_b"):
    KEYS[name] = len(KEYS)
for half in range(2):
    for name in ("z1", "x1", "bz1", "bx1", "z2", "x2", "bz2", "bx2", "z3", "x3"):
        KEYS[name, half] = len(KEYS)


def kernel(
    rows,
    reps,
    halves,
    scale,
    tile_rows,
    tile_cols,
    basis_far,
    precond_far,
    tiles_far,
    directions,
    projected,
    request,
    codes,
    basis,
    precond,
    tiles,
    wanted,
    wants,
    base,
    weight,
    weight_sz,
    weight_sx,
    weight_rz,
    weight_rx,
    sz1,
    sx1,
    rz1,
    rx1a,
    rx1b,
    sz2,
    sx2,
    rz2,
    rx2a,
    rx2b,
    sz3,
    sx3,
    rz3,
    rx3a,
    rx3b,
    prod_i1,
    prod_i2,
    prod_j1,
    prod_j2,
    tx1,
    tx2,
    bz1,
    bx1,
    bz2,
    bx2,
    diag,
    applied,
    right,
    seed,
    updated,
    low_m,
    low_a,
    low_b,
    low_c,
    low_piece,
    low,
    mid_m,
    mid_a,
    mid_n,
    mid_b,
    new_m,
    new_a,
    new_b,
    new_c,
    new_piece,
    new,
    end_m,
    end_a,
    end_n,
    end_b,
    send,
    recv,
    local,
):
    rx1, rx2, rx3 = (rx1a, rx1b), (rx2a, rx2b), (rx3a, rx3b)
    row = lax.axis_index("row")
    rep = lax.axis_index("rep")
    chips = rows // 2
    each = base.shape[0]
    size = base.shape[2]
    count = base.shape[1]
    z_slots = 2 * chips
    x_slots = 2 * (reps - 1)
    side = math.isqrt(reps)
    chip = row // 2
    core = lax.rem(row, 2)
    part = count // halves

    barrier = pltpu.get_barrier_semaphore()
    for d in range(1, rows):
        pl.semaphore_signal(
            barrier, inc=1, device_id={"row": lax.rem(row + d, rows)}, device_id_type=MESH
        )
    for d in range(1, reps):
        pl.semaphore_signal(
            barrier, inc=1, device_id={"rep": lax.rem(rep + d, reps)}, device_id_type=MESH
        )

    basis_load = pltpu.make_async_copy(basis_far, basis, local.at[3])
    precond_load = pltpu.make_async_copy(precond_far, precond, local.at[4])
    basis_load.start()
    precond_load.start()
    diag_load = pltpu.make_async_copy(
        tiles_far.at[pl.ds(0, each)], tiles.at[pl.ds(0, each)], local.at[0]
    )
    rest = tiles.shape[0] - each
    other_load = pltpu.make_async_copy(
        tiles_far.at[pl.ds(each, rest)], tiles.at[pl.ds(each, rest)], local.at[1]
    )
    diag_load.start()
    other_load.start()

    def z_holder(delta):
        half = chips // 2
        if delta == 0:
            other = 1 - core
        elif delta < half:
            other = core
        elif delta > half:
            other = 1 - core
        else:
            other = jnp.where(chip < half, core, 1 - core)
        return {"row": lax.rem(chip + delta, chips) * 2 + other}

    def z_reader(delta):
        half = chips // 2
        there = lax.rem(chip - delta + chips, chips)
        if delta == 0:
            other = 1 - core
        elif delta < half:
            other = core
        elif delta > half:
            other = 1 - core
        else:
            other = jnp.where(there < half, core, 1 - core)
        return {"row": there * 2 + other}

    def x_holder(sigma):
        across = lax.rem(rep // side + sigma // side, side)
        along = lax.rem(lax.rem(rep, side) + sigma % side, side)
        return {"rep": across * side + along}

    def x_reader(sigma):
        across = lax.rem(rep // side - sigma // side + side, side)
        along = lax.rem(lax.rem(rep, side) - sigma % side + side, side)
        return {"rep": across * side + along}

    def push(source, target, key, device):
        pltpu.make_async_remote_copy(
            src_ref=source,
            dst_ref=target,
            send_sem=send.at[KEYS[key]],
            recv_sem=recv.at[KEYS[key]],
            device_id=device,
            device_id_type=MESH,
        ).start()

    def landed(buffer, key):
        pltpu.make_async_copy(buffer, buffer, recv.at[KEYS[key]]).wait()

    def gone(buffer, key):
        pltpu.make_async_copy(buffer, buffer, send.at[KEYS[key]]).wait()

    def scatter(full, slots, key):
        for d in range(1, rows):
            to = lax.rem(row + d, rows)
            push(full.at[to], slots.at[row], key, {"row": to})
        pltpu.make_async_copy(full.at[row], slots.at[row], recv.at[KEYS[key]]).start()

    def spread(source, slots, key, axis):
        if axis == "row":
            me, length = row, rows
        else:
            me, length = rep, reps
        for d in range(1, length):
            push(source, slots.at[me], key, {axis: lax.rem(me + d, length)})
        pltpu.make_async_copy(source, slots.at[me], recv.at[KEYS[key]]).start()

    def total(slots):
        value = slots[0]
        for i in range(1, slots.shape[0]):
            value = value + slots[i]
        return value

    def cut(value, full):
        lines = full.shape[1]
        for i in range(full.shape[0]):
            full[i] = value[i * lines : (i + 1) * lines, :]

    def joined(slots, whole):
        lines = slots.shape[1]
        for i in range(slots.shape[0]):
            whole[i * lines : (i + 1) * lines, :] = slots[i]

    def scaled(block, scaling):
        return jnp.concatenate([block.astype(BF16), *split(block * scaling)], axis=0)

    table = request_table(tile_rows[...], tile_cols[...], row, rep, each, rows, reps)
    for peer in range(request.shape[0]):
        request[peer] = table[2 * peer : 2 * peer + 2]
    basis_load.wait()
    precond_load.wait()
    own_low = jnp.zeros((count, 3 * count), F32)
    for t in range(each):
        block = basis[:, t * size : (t + 1) * size]
        base[t] = block.astype(F32)
        weight[t] = precond[:, t * size : (t + 1) * size]
        own_low = own_low + dot_t(block, scaled(base[t], weight[t]))
    own_low = own_low * scale
    own_low = jnp.concatenate(
        [own_low[:, :count], own_low[:, count : 2 * count] + own_low[:, 2 * count :]], axis=1
    )
    cut(jnp.concatenate([own_low[: count // 2], own_low[count // 2 :]], axis=1), low_m)

    pl.semaphore_wait(barrier, rows + reps - 2)

    for delta in range(chips):
        push(request.at[delta], wanted.at[delta], "request", z_holder(delta))
    for sigma in range(1, reps):
        here = chips + sigma - 1
        push(request.at[here], wanted.at[here], "request", x_holder(sigma))
    scatter(low_m, low_a, "low_a")
    code_load = pltpu.make_async_copy(request, codes, local.at[5])
    code_load.start()

    diag_load.wait()
    for t in range(each):
        diag[t] = dot_t(basis[:, t * size : (t + 1) * size], tiles[t])

    landed(wanted, "request")
    to_scalars = pltpu.make_async_copy(wanted, wants, local.at[2])
    to_scalars.start()
    to_scalars.wait()
    code_load.wait()
    landed(low_a, "low_a")
    low_piece[0] = total(low_a)
    spread(low_piece.at[0], low_b, "low_b", "rep")

    def rows_of(half):
        return slice(half * part, (half + 1) * part)

    def z_asked(slot):
        return lax.shift_right_logical(wants[slot // 2, slot % 2, 0], 16) & (each - 1)

    def x_asked(slot):
        return lax.shift_right_logical(wants[chips + slot // 2, slot % 2, 0], 16) & (each - 1)

    def far(size_of, index):
        return -min(index, size_of - index)

    z_order = sorted(range(chips), key=lambda delta: far(chips, delta))
    x_order = sorted(
        range(1, reps), key=lambda sigma: far(side, sigma // side) + far(side, sigma % side)
    )

    def answer(own, to_z, to_x, from_z, from_x, turn, half):
        here = rows_of(half)
        for slot in range(z_slots):
            from_z[half, slot] = own[z_asked(slot), here, :]
        for slot in range(x_slots):
            from_x[half, slot] = own[x_asked(slot), here, :]
        z_left, x_left = list(z_order), list(x_order)
        while z_left or x_left:
            for sigma in x_left[:2]:
                block = pl.ds(2 * (sigma - 1), 2)
                push(
                    from_x.at[half, block], to_x[half].at[block], ("x" + turn, half), x_reader(sigma)
                )
            for delta in z_left[:1]:
                block = pl.ds(2 * delta, 2)
                push(
                    from_z.at[half, block], to_z.at[half, block], ("z" + turn, half), z_reader(delta)
                )
            z_left, x_left = z_left[1:], x_left[2:]

    def z_code(slot):
        return codes[slot // 2, slot % 2, 0]

    def tile_of(slot):
        return tiles[jnp.minimum(z_code(slot) & 255, tiles.shape[0] - 1)]

    def x_of(slot):
        return jnp.minimum(lax.shift_right_logical(z_code(slot), 8) & 255, x_slots - 1)

    def x_source(slot):
        return jnp.minimum(codes[chips + slot // 2, slot % 2, 0] & 255, z_slots - 1)

    def returned(forward, backward, images, mirrored, packed, to_z, to_x, turn, half):
        for slot in range(z_slots):
            images[half, slot] = forward(slot)
        for slot in range(x_slots):
            packed[half, slot] = images[half, x_source(slot)]
        for sigma in x_order:
            block = pl.ds(2 * (sigma - 1), 2)
            push(
                packed.at[half, block], to_x.at[half, block], ("bx" + turn, half), x_holder(sigma)
            )
        for delta in z_order[:-1]:
            for slot in (2 * delta, 2 * delta + 1):
                mirrored[half, slot] = backward(slot)
            block = pl.ds(2 * delta, 2)
            push(
                mirrored.at[half, block], to_z.at[half, block], ("bz" + turn, half), z_holder(delta)
            )

    inner = pl.ds(2, z_slots - 2)

    def summed(from_z, from_x, target, half):
        def strip(index, carry):
            here = pl.ds(pl.multiple_of(index * 8, 8), 8)
            there = pl.ds(pl.multiple_of(half * part + index * 8, 8), 8)
            totals = [diag[t, there, :] for t in range(each)]
            slots = [(from_z, slot, slot // 2, slot % 2) for slot in range(2, z_slots)]
            slots += [(from_x, slot, chips + slot // 2, slot % 2) for slot in range(x_slots)]
            for source, slot, peer, place in slots:
                value = source[half, slot, here, :]
                asked = lax.shift_right_logical(wanted[peer, place : place + 1, :], 16) & 255
                for t in range(each):
                    hit = jnp.broadcast_to(asked == t, (8, 128))
                    hit = jnp.concatenate([hit] * (size // 128), axis=1)
                    totals[t] = totals[t] + jnp.where(hit, value, 0.0)
            for t in range(each):
                target[t, there, :] = totals[t]
            return carry

        lax.fori_loop(0, part // 8, strip, 0)

    def all_rows(buffer, slot):
        return jnp.concatenate([buffer[half, slot] for half in range(halves)], axis=0)

    def rows_held(buffers, slot):
        return jnp.concatenate([buffer[slot] for buffer in buffers], axis=0)

    for half in range(halves):
        answer(base, rz1, rx1, sz1, sx1, "1", half)
    for slot in range(z_slots):
        weight_sz[slot] = weight[z_asked(slot)]
    for slot in range(x_slots):
        weight_sx[slot] = weight[x_asked(slot)]
    for delta in range(chips):
        block = pl.ds(2 * delta, 2)
        push(weight_sz.at[block], weight_rz.at[block], "weight_z", z_reader(delta))
    for sigma in range(1, reps):
        block = pl.ds(2 * (sigma - 1), 2)
        push(weight_sx.at[block], weight_rx.at[block], "weight_x", x_reader(sigma))
    own_mid = jnp.zeros((2 * count, 3 * count), F32)
    for t in range(each):
        own_mid = own_mid + dot_t(stacked(diag[t]), scaled(base[t], weight[t]))
    other_load.wait()
    for half in range(halves):
        landed(rz1.at[half], ("z1", half))
        landed(rx1[half], ("x1", half))
        if half == 0:
            landed(low_b, "low_b")
            low_piece[1] = total(low_b)
            spread(low_piece.at[1], low_c, "low_c", "row")
        returned(
            lambda slot: dot_t(rz1[half, slot].astype(BF16), tile_of(slot)),
            lambda slot: dot(rx1[half][x_of(slot)].astype(BF16), tile_of(slot)),
            prod_i1,
            prod_j1,
            tx1,
            bz1,
            bx1,
            "1",
            half,
        )
    landed(low_c, "low_c")
    joined(low_c, low)
    landed(weight_rz, "weight_z")
    landed(weight_rx, "weight_x")

    def used(slot):
        return z_code(slot) >= 16777216

    own_form = own_mid[:, :count]
    both_form = jnp.zeros((2 * count, count), F32)
    scaled_form = own_mid[:, count : 2 * count] + own_mid[:, 2 * count :]
    for slot in range(z_slots):
        there = x_of(slot)
        product = dot_t(
            stacked(all_rows(prod_i1, slot)), scaled(rows_held(rx1, there), weight_rx[there])
        )
        product = jnp.where(used(slot), product, 0.0)
        if slot < 2:
            own_form = own_form + product[:, :count]
        else:
            both_form = both_form + product[:, :count]
        scaled_form = scaled_form + product[:, count : 2 * count] + product[:, 2 * count :]
        if slot >= 2:
            product = dot_t(
                stacked(all_rows(prod_j1, slot)),
                stacked(all_rows(rz1, slot) * weight_rz[slot]),
            )
            product = jnp.where(used(slot), product, 0.0)
            scaled_form = scaled_form + product[:, :count] + product[:, count:]
    both_form = folded(both_form + 0.5 * own_form)
    scaled_form = folded(scaled_form)
    quarter = jnp.concatenate([both_form, scaled_form], axis=1) * scale
    mid_m[...] = jnp.concatenate([quarter[: count // 2], quarter[count // 2 :]], axis=1)
    spread(mid_m, mid_a, "mid_a", "rep")

    for half in range(halves):
        landed(bz1.at[half, inner], ("bz1", half))
        landed(bx1.at[half], ("bx1", half))
        summed(bz1, bx1, applied, half)
        if half == halves - 1:
            landed(mid_a, "mid_a")
            mid_n[...] = total(mid_a)
            spread(mid_n, mid_b, "mid_b", "row")
        answer(applied, rz2, rx2, sz2, sx2, "2", half)
    landed(mid_b, "mid_b")
    quarter = total(mid_b)
    quarter = jnp.concatenate([quarter[:, : 2 * count], quarter[:, 2 * count :]], axis=0)
    basis_applied = quarter[:, :count] + quarter[:, :count].T
    scaled_applied = quarter[:, count:]
    basis_gram = jnp.concatenate([low[:, :count], low[:, 2 * count : 3 * count]], axis=0)
    scaled_gram = jnp.concatenate([low[:, count : 2 * count], low[:, 3 * count :]], axis=0)
    row_of = lax.broadcasted_iota(jnp.int32, (count, count), 0)
    col_of = lax.broadcasted_iota(jnp.int32, (count, count), 1)
    ritz = jnp.sum(jnp.where(row_of == col_of, basis_applied, 0.0), axis=1, keepdims=True)
    correlation = basis_applied - ritz * basis_gram
    mixed = correlation + jnp.where(row_of == col_of, ritz, 0.0)
    coefficients = exact(mixed, scaled_gram) - scaled_applied

    for half in range(halves):
        here = rows_of(half)
        both = stacked(jnp.concatenate([mixed[here], coefficients[here]], axis=0))

        def rebuilt(block, image, scaling):
            parts = folded(dot(both, block.astype(BF16)))
            remainder = parts[:part] - image
            return scaling * remainder - parts[part:], remainder

        def forward(slot):
            value, unused = rebuilt(all_rows(rz1, slot), rz2[half, slot], weight_rz[slot])
            return folded(dot_t(stacked(value), tile_of(slot)))

        def backward(slot):
            there = x_of(slot)
            value, unused = rebuilt(rows_held(rx1, there), rx2[half][there], weight_rx[there])
            return folded(dot(stacked(value), tile_of(slot)))

        landed(rz2.at[half], ("z2", half))
        landed(rx2[half], ("x2", half))
        returned(forward, backward, prod_i2, prod_j2, tx2, bz2, bx2, "2", half)
        for t in range(each):
            value, remainder = rebuilt(base[t], applied[t, here, :], weight[t])
            seed[t, here, :] = value
            right[t, here, :] = remainder
            diag[t, here, :] = folded(dot_t(stacked(value), tiles[t]))

    for half in range(halves):
        here = rows_of(half)
        landed(bz2.at[half, inner], ("bz2", half))
        landed(bx2.at[half], ("bx2", half))
        summed(bz2, bx2, updated, half)
        for t in range(each):
            value = seed[t, here, :]
            updated[t, here, :] = value + weight[t] * (
                right[t, here, :] - (updated[t, here, :] - ritz[here] * value)
            )
        if half == halves - 1:
            second = jnp.zeros((2 * count, 5 * count), F32)
            for t in range(each):
                parts = split(updated[t])
                second = second + dot_t(
                    jnp.concatenate(parts, axis=0),
                    jnp.concatenate([*parts, base[t].astype(BF16), *split(applied[t])], axis=0),
                )
            second = folded(second) * scale
            second = jnp.concatenate(
                [
                    second[:, :count] + second[:, count : 2 * count],
                    second[:, 2 * count : 3 * count],
                    second[:, 3 * count : 4 * count] + second[:, 4 * count :],
                    jnp.zeros((count, count), F32),
                ],
                axis=1,
            )
            cut(second, new_m)
            scatter(new_m, new_a, "new_a")
        answer(updated, rz3, rx3, sz3, sx3, "3", half)
    form = jnp.zeros((2 * count, 2 * count), F32)
    for t in range(each):
        value = stacked(updated[t])
        form = form + dot_t(value, stacked(folded(dot_t(value, tiles[t]))))
    form = 0.5 * form
    landed(new_a, "new_a")
    new_piece[0] = total(new_a)
    spread(new_piece.at[0], new_b, "new_b", "rep")
    for half in range(halves):
        landed(rz3.at[half], ("z3", half))
        landed(rx3[half], ("x3", half))
        if half == halves - 1:
            landed(new_b, "new_b")
            new_piece[1] = total(new_b)
            spread(new_piece.at[1], new_c, "new_c", "row")
        for slot in range(z_slots):
            prod_i2[half, slot] = folded(dot_t(stacked(rz3[half, slot]), tile_of(slot)))
    for slot in range(z_slots):
        product = dot_t(stacked(rows_held(rx3, x_of(slot))), stacked(all_rows(prod_i2, slot)))
        form = form + jnp.where(used(slot), 0.5 if slot < 2 else 1.0, 0.0) * product
    form = folded(form)
    form = (form[:, :count] + form[:, count:]) * scale
    lines = count // 4
    end_m[...] = jnp.concatenate([form[i * lines : (i + 1) * lines] for i in range(4)], axis=1)
    spread(end_m, end_a, "end_a", "row")

    landed(new_c, "new_c")
    joined(new_c, new)
    new_gram = new[:, :count]
    overlap = new[:, count : 2 * count]
    new_applied = new[:, 2 * count : 3 * count]
    identity = (row_of == col_of).astype(F32)
    correction_gram = new_gram - exact_t(exact(overlap, 2.0 * identity - basis_gram), overlap)
    work = eliminated(jnp.concatenate([correction_gram, identity], axis=1), 0, count // 2)
    landed(end_a, "end_a")
    end_n[...] = total(end_a)
    spread(end_n, end_b, "end_b", "rep")
    inverse = eliminated(work, count // 2, count)[:, count:]
    turned = exact(overlap, basis_applied)
    cross = new_applied - turned
    known = exact_t(new_applied, overlap)
    known = exact_t(turned, overlap) - known - exact_t(overlap, new_applied)
    projected[:count, :count] = basis_applied
    projected[count:, :count] = exact(inverse, cross)
    projected[:count, count:] = exact_t(cross.T, inverse)
    for t in range(each):
        value = updated[t] - folded(dot(stacked(overlap), base[t].astype(BF16)))
        directions[:, t * size : (t + 1) * size] = exact(inverse, value)
    landed(end_b, "end_b")
    form = total(end_b)
    form = jnp.concatenate([form[:, i * count : (i + 1) * count] for i in range(4)], axis=0)
    middle = form + form.T + known
    projected[count:, count:] = exact_t(exact(inverse, middle), inverse)

    gone(request, "request")
    gone(weight_sz, "weight_z")
    gone(weight_sx, "weight_x")
    for half in range(halves):
        for turn, from_z, from_x in (("1", sz1, sx1), ("2", sz2, sx2), ("3", sz3, sx3)):
            gone(from_z.at[half], ("z" + turn, half))
            gone(from_x.at[half], ("x" + turn, half))
        for turn, from_z, from_x in (("1", prod_j1, tx1), ("2", prod_j2, tx2)):
            gone(from_z.at[half, inner], ("bz" + turn, half))
            gone(from_x.at[half], ("bx" + turn, half))
    other_rows = pl.ds(0, rows - 1)
    other_reps = pl.ds(0, reps - 1)
    for key, buffer in (
        ("low_a", low_a.at[other_rows]),
        ("low_b", low_b.at[other_reps]),
        ("low_c", low_c.at[other_rows]),
        ("mid_a", mid_a.at[other_reps]),
        ("mid_b", mid_b.at[other_rows]),
        ("new_a", new_a.at[other_rows]),
        ("new_b", new_b.at[other_reps]),
        ("new_c", new_c.at[other_rows]),
        ("end_a", end_a.at[other_rows]),
        ("end_b", end_b.at[other_reps]),
    ):
        gone(buffer, key)


def publish(directions, projected, directions_out, projected_out):
    directions_out[...] = directions[...]
    projected_out[...] = projected[...]


def shards(basis, precond, tiles, tile_rows, tile_cols):
    count, shard = basis.shape
    size = tiles.shape[1]
    each = shard // size
    rows = lax.axis_size("row")
    reps = lax.axis_size("rep")
    chips = rows // 2
    halves = 2
    asked = (chips + reps - 1, 2, 128)
    z_slots = 2 * chips
    x_slots = 2 * (reps - 1)

    def held(*shape):
        return pltpu.VMEM(shape, F32)

    z_block = held(halves, z_slots, count // halves, size)
    x_block = held(halves, x_slots, count // halves, size)
    x_half = held(x_slots, count // halves, size)
    own = held(each, count, size)
    wide = 4 * count
    lines = count // rows
    scratch = [
        pltpu.VMEM(asked, jnp.int32),
        pltpu.SMEM(asked, jnp.int32),
        pltpu.VMEM(basis.shape, BF16),
        held(1, shard),
        pltpu.VMEM(tiles.shape, BF16),
        pltpu.VMEM(asked, jnp.int32),
        pltpu.SMEM(asked, jnp.int32),
        own,
        held(each, 1, size),
        held(z_slots, 1, size),
        held(x_slots, 1, size),
        held(z_slots, 1, size),
        held(x_slots, 1, size),
        *([z_block, x_block, z_block, *([x_half] * halves)] * 3),
        z_block,
        z_block,
        z_block,
        z_block,
        x_block,
        x_block,
        z_block,
        x_block,
        z_block,
        x_block,
        *([own] * 5),
        held(rows, lines // 2, wide),
        held(rows, lines // 2, wide),
        held(reps, lines // 2, wide),
        held(rows, lines // 2, wide),
        held(2, lines // 2, wide),
        held(count // 2, wide),
        held(count // 2, wide),
        held(reps, count // 2, wide),
        held(count // 2, wide),
        held(rows, count // 2, wide),
        held(rows, lines, wide),
        held(rows, lines, wide),
        held(reps, lines, wide),
        held(rows, lines, wide),
        held(2, lines, wide),
        held(count, wide),
        held(count // 4, wide),
        held(rows, count // 4, wide),
        held(count // 4, wide),
        held(reps, count // 4, wide),
        pltpu.SemaphoreType.DMA((len(KEYS),)),
        pltpu.SemaphoreType.DMA((len(KEYS),)),
        pltpu.SemaphoreType.DMA((6,)),
    ]
    vmem = pl.BlockSpec(memory_space=pltpu.VMEM)
    far_away = pl.BlockSpec(memory_space=pl.ANY)
    found = pl.pallas_call(
        functools.partial(kernel, rows, reps, halves, 1.0 / (shard * rows * reps)),
        name="davidson_step",
        out_shape=(
            jax.ShapeDtypeStruct((count, shard), F32),
            jax.ShapeDtypeStruct((2 * count, 2 * count), F32),
        ),
        in_specs=[vmem, vmem, far_away, far_away, far_away],
        out_specs=(vmem, vmem),
        scratch_shapes=scratch,
        compiler_params=pltpu.CompilerParams(
            collective_id=0, has_side_effects=True, vmem_limit_bytes=60 * 1024 * 1024
        ),
    )(
        tile_rows.reshape(1, tile_rows.shape[0]),
        tile_cols.reshape(1, tile_cols.shape[0]),
        basis,
        precond.reshape(1, shard),
        tiles,
    )
    return pl.pallas_call(
        publish,
        name="publish",
        out_shape=tuple(jax.ShapeDtypeStruct(a.shape, a.dtype) for a in found),
        in_specs=[vmem, vmem],
        out_specs=(vmem, vmem),
    )(*found)


def solution(mesh):
    both = ("row", "rep")
    placed = (P(None, both), P(both), P(both, None, None), P(both), P(both))
    return jax.shard_map(
        shards, mesh=mesh, in_specs=placed, out_specs=(P(None, both), P()), check_vma=False
    )
```

```python
import functools
import math
import jax
import jax.numpy as jnp
from jax import lax
from jax.experimental import pallas as pl
from jax.experimental.pallas import tpu as pltpu
from jax.sharding import PartitionSpec as P

MESH = pl.DeviceIdType.MESH
F32 = jnp.float32
BF16 = jnp.bfloat16
HIGHEST = lax.Precision.HIGHEST


def request_table(tile_rows, tile_cols, row, rep, each, rows, reps):
    entries = tile_rows.shape[1]
    chips = rows // 2
    side = math.isqrt(reps)
    bits = each.bit_length() - 1
    side_bits = side.bit_length() - 1
    place = lax.broadcasted_iota(jnp.int32, (1, entries), 1)
    col_peer = lax.shift_right_logical(tile_cols, bits)
    row_peer = lax.shift_right_logical(tile_rows, bits)
    delta = (lax.shift_right_logical(col_peer, 1) - row // 2 + chips) & (chips - 1)
    limit = chips // 2 + jnp.where(row // 2 < chips // 2, 1, 0)
    differs = (col_peer & 1) ^ lax.rem(row, 2)
    crossed = jnp.where(delta < limit, 0, 1)
    chosen = ((delta == 0) | (differs == crossed)) & (place >= each)
    col_key = jnp.where(chosen, col_peer, -1)
    row_key = jnp.where(chosen, row_peer, -1)
    first = lax.broadcasted_iota(jnp.int32, (entries, entries), 0)
    second = lax.broadcasted_iota(jnp.int32, (entries, entries), 1)

    def rank(key):
        upright = jnp.sum(jnp.where(first == second, key, 0), axis=1, keepdims=True)
        return jnp.sum(
            jnp.where((first < second) & (upright == key), 1, 0), axis=0, keepdims=True
        )

    across = (lax.shift_right_logical(row_peer, side_bits) - rep // side + side) & (side - 1)
    along = ((row_peer & (side - 1)) - lax.rem(rep, side) + side) & (side - 1)
    z_slot = 2 * delta + rank(col_key)
    x_slot = 2 * (across * side + along - 1) + rank(row_key)
    z_code = place + x_slot * 256 + (tile_cols & (each - 1)) * 65536 + 16777216
    x_code = z_slot + (tile_rows & (each - 1)) * 65536 + 16777216
    z_slot = jnp.where(chosen, z_slot, -1)
    x_slot = jnp.where(chosen, x_slot + 2 * chips, -1)
    slots = lax.broadcasted_iota(jnp.int32, (2 * (chips + reps), entries), 0)
    code = jnp.where(slots == z_slot, z_code, 0) + jnp.where(slots == x_slot, x_code, 0)
    code = jnp.sum(code, axis=1, keepdims=True)
    return jnp.broadcast_to(jnp.where(code == 0, each * 65536, code), (code.shape[0], 128))


def split(x):
    high = x.astype(BF16)
    low = (x - high.astype(F32)).astype(BF16)
    return high, low


def stacked(x):
    return jnp.concatenate(split(x), axis=0)


def folded(x):
    half = x.shape[0] // 2
    return x[:half] + x[half:]


def dot(a, b):
    return lax.dot_general(a, b, (((1,), (0,)), ((), ())), preferred_element_type=F32)


def dot_t(a, b):
    return lax.dot_general(a, b, (((1,), (1,)), ((), ())), preferred_element_type=F32)


def exact(a, b):
    return lax.dot_general(
        a, b, (((1,), (0,)), ((), ())), precision=HIGHEST, preferred_element_type=F32
    )


def exact_t(a, b):
    return lax.dot_general(
        a, b, (((1,), (1,)), ((), ())), precision=HIGHEST, preferred_element_type=F32
    )


def eliminated(work, begin, end):
    which = lax.broadcasted_iota(jnp.int32, (work.shape[0], 1), 0)
    for j in range(begin, end):
        scale = lax.rsqrt(work[j : j + 1, j : j + 1])
        pivot = work[j : j + 1, :] * scale
        ratio = work[:, j : j + 1] * scale
        work = jnp.where(
            which == j, pivot, work - jnp.where(which > j, ratio, 0.0) * pivot
        )
    return work


KEYS = {}
for name in ("request", "weight_z", "weight_x", "low_a", "low_b", "low_c", "mid_a", "mid_b"):
    KEYS[name] = len(KEYS)
for name in ("new_a", "new_b", "new_c", "end_a", "end_b"):
    KEYS[name] = len(KEYS)
for half in range(2):
    for name in ("z1", "x1", "bz1", "bx1", "z2", "x2", "bz2", "bx2", "z3", "x3"):
        KEYS[name, half] = len(KEYS)


def kernel(
    rows,
    reps,
    halves,
    scale,
    tile_rows,
    tile_cols,
    basis_far,
    precond_far,
    tiles_far,
    directions,
    projected,
    request,
    codes,
    basis,
    precond,
    tiles,
    wanted,
    wants,
    base,
    weight,
    weight_sz,
    weight_sx,
    weight_rz,
    weight_rx,
    sz1,
    sx1,
    rz1,
    rx1a,
    rx1b,
    sz2,
    sx2,
    rz2,
    rx2a,
    rx2b,
    sz3,
    sx3,
    rz3,
    rx3a,
    rx3b,
    prod_i1,
    prod_i2,
    prod_j1,
    prod_j2,
    tx1,
    tx2,
    bz1,
    bx1,
    bz2,
    bx2,
    diag,
    applied,
    right,
    seed,
    updated,
    low_m,
    low_a,
    low_b,
    low_c,
    low_piece,
    low,
    mid_m,
    mid_a,
    mid_n,
    mid_b,
    new_m,
    new_a,
    new_b,
    new_c,
    new_piece,
    new,
    end_m,
    end_a,
    end_n,
    end_b,
    send,
    recv,
    local,
):
    rx1, rx2, rx3 = (rx1a, rx1b), (rx2a, rx2b), (rx3a, rx3b)
    row = lax.axis_index("row")
    rep = lax.axis_index("rep")
    chips = rows // 2
    each = base.shape[0]
    size = base.shape[2]
    count = base.shape[1]
    z_slots = 2 * chips
    x_slots = 2 * (reps - 1)
    side = math.isqrt(reps)
    chip = row // 2
    core = lax.rem(row, 2)
    part = count // halves

    barrier = pltpu.get_barrier_semaphore()
    for d in range(1, rows):
        pl.semaphore_signal(
            barrier, inc=1, device_id={"row": lax.rem(row + d, rows)}, device_id_type=MESH
        )
    for d in range(1, reps):
        pl.semaphore_signal(
            barrier, inc=1, device_id={"rep": lax.rem(rep + d, reps)}, device_id_type=MESH
        )

    basis_load = pltpu.make_async_copy(basis_far, basis, local.at[3])
    precond_load = pltpu.make_async_copy(precond_far, precond, local.at[4])
    basis_load.start()
    precond_load.start()
    diag_load = pltpu.make_async_copy(
        tiles_far.at[pl.ds(0, each)], tiles.at[pl.ds(0, each)], local.at[0]
    )
    rest = tiles.shape[0] - each
    other_load = pltpu.make_async_copy(
        tiles_far.at[pl.ds(each, rest)], tiles.at[pl.ds(each, rest)], local.at[1]
    )
    diag_load.start()
    other_load.start()

    def z_holder(delta):
        half = chips // 2
        if delta == 0:
            other = 1 - core
        elif delta < half:
            other = core
        elif delta > half:
            other = 1 - core
        else:
            other = jnp.where(chip < half, core, 1 - core)
        return {"row": lax.rem(chip + delta, chips) * 2 + other}

    def z_reader(delta):
        half = chips // 2
        there = lax.rem(chip - delta + chips, chips)
        if delta == 0:
            other = 1 - core
        elif delta < half:
            other = core
        elif delta > half:
            other = 1 - core
        else:
            other = jnp.where(there < half, core, 1 - core)
        return {"row": there * 2 + other}

    def x_holder(sigma):
        across = lax.rem(rep // side + sigma // side, side)
        along = lax.rem(lax.rem(rep, side) + sigma % side, side)
        return {"rep": across * side + along}

    def x_reader(sigma):
        across = lax.rem(rep // side - sigma // side + side, side)
        along = lax.rem(lax.rem(rep, side) - sigma % side + side, side)
        return {"rep": across * side + along}

    def push(source, target, key, device):
        pltpu.make_async_remote_copy(
            src_ref=source,
            dst_ref=target,
            send_sem=send.at[KEYS[key]],
            recv_sem=recv.at[KEYS[key]],
            device_id=device,
            device_id_type=MESH,
        ).start()

    def landed(buffer, key):
        pltpu.make_async_copy(buffer, buffer, recv.at[KEYS[key]]).wait()

    def gone(buffer, key):
        pltpu.make_async_copy(buffer, buffer, send.at[KEYS[key]]).wait()

    def scatter(full, slots, key):
        for d in range(1, rows):
            to = lax.rem(row + d, rows)
            push(full.at[to], slots.at[row], key, {"row": to})
        pltpu.make_async_copy(full.at[row], slots.at[row], recv.at[KEYS[key]]).start()

    def spread(source, slots, key, axis):
        if axis == "row":
            me, length = row, rows
        else:
            me, length = rep, reps
        for d in range(1, length):
            push(source, slots.at[me], key, {axis: lax.rem(me + d, length)})
        pltpu.make_async_copy(source, slots.at[me], recv.at[KEYS[key]]).start()

    def total(slots):
        value = slots[0]
        for i in range(1, slots.shape[0]):
            value = value + slots[i]
        return value

    def cut(value, full):
        lines = full.shape[1]
        for i in range(full.shape[0]):
            full[i] = value[i * lines : (i + 1) * lines, :]

    def joined(slots, whole):
        lines = slots.shape[1]
        for i in range(slots.shape[0]):
            whole[i * lines : (i + 1) * lines, :] = slots[i]

    def scaled(block, scaling):
        return jnp.concatenate([block.astype(BF16), *split(block * scaling)], axis=0)

    table = request_table(tile_rows[...], tile_cols[...], row, rep, each, rows, reps)
    for peer in range(request.shape[0]):
        request[peer] = table[2 * peer : 2 * peer + 2]
    basis_load.wait()
    precond_load.wait()
    own_low = jnp.zeros((count, 3 * count), F32)
    for t in range(each):
        block = basis[:, t * size : (t + 1) * size]
        base[t] = block.astype(F32)
        weight[t] = precond[:, t * size : (t + 1) * size]
        own_low = own_low + dot_t(block, scaled(base[t], weight[t]))
    own_low = own_low * scale
    own_low = jnp.concatenate(
        [own_low[:, :count], own_low[:, count : 2 * count] + own_low[:, 2 * count :]], axis=1
    )
    cut(jnp.concatenate([own_low[: count // 2], own_low[count // 2 :]], axis=1), low_m)

    pl.semaphore_wait(barrier, rows + reps - 2)

    for delta in range(chips):
        push(request.at[delta], wanted.at[delta], "request", z_holder(delta))
    for sigma in range(1, reps):
        here = chips + sigma - 1
        push(request.at[here], wanted.at[here], "request", x_holder(sigma))
    scatter(low_m, low_a, "low_a")
    code_load = pltpu.make_async_copy(request, codes, local.at[5])
    code_load.start()

    diag_load.wait()
    for t in range(each):
        diag[t] = dot_t(basis[:, t * size : (t + 1) * size], tiles[t])

    landed(wanted, "request")
    to_scalars = pltpu.make_async_copy(wanted, wants, local.at[2])
    to_scalars.start()
    to_scalars.wait()
    code_load.wait()
    landed(low_a, "low_a")
    low_piece[0] = total(low_a)
    spread(low_piece.at[0], low_b, "low_b", "rep")

    def rows_of(half):
        return slice(half * part, (half + 1) * part)

    def z_asked(slot):
        return lax.shift_right_logical(wants[slot // 2, slot % 2, 0], 16) & (each - 1)

    def x_asked(slot):
        return lax.shift_right_logical(wants[chips + slot // 2, slot % 2, 0], 16) & (each - 1)

    def far(size_of, index):
        return -min(index, size_of - index)

    z_order = sorted(range(chips), key=lambda delta: far(chips, delta))
    x_order = sorted(
        range(1, reps), key=lambda sigma: far(side, sigma // side) + far(side, sigma % side)
    )

    def answer(own, to_z, to_x, from_z, from_x, turn, half):
        here = rows_of(half)
        for slot in range(z_slots):
            from_z[half, slot] = own[z_asked(slot), here, :]
        for slot in range(x_slots):
            from_x[half, slot] = own[x_asked(slot), here, :]
        z_left, x_left = list(z_order), list(x_order)
        while z_left or x_left:
            for sigma in x_left[:2]:
                block = pl.ds(2 * (sigma - 1), 2)
                push(
                    from_x.at[half, block], to_x[half].at[block], ("x" + turn, half), x_reader(sigma)
                )
            for delta in z_left[:1]:
                block = pl.ds(2 * delta, 2)
                push(
                    from_z.at[half, block], to_z.at[half, block], ("z" + turn, half), z_reader(delta)
                )
            z_left, x_left = z_left[1:], x_left[2:]

    def z_code(slot):
        return codes[slot // 2, slot % 2, 0]

    def tile_of(slot):
        return tiles[jnp.minimum(z_code(slot) & 255, tiles.shape[0] - 1)]

    def x_of(slot):
        return jnp.minimum(lax.shift_right_logical(z_code(slot), 8) & 255, x_slots - 1)

    def x_source(slot):
        return jnp.minimum(codes[chips + slot // 2, slot % 2, 0] & 255, z_slots - 1)

    def returned(forward, backward, images, mirrored, packed, to_z, to_x, turn, half):
        for slot in range(z_slots):
            images[half, slot] = forward(slot)
        for slot in range(x_slots):
            packed[half, slot] = images[half, x_source(slot)]
        for sigma in x_order:
            block = pl.ds(2 * (sigma - 1), 2)
            push(
                packed.at[half, block], to_x.at[half, block], ("bx" + turn, half), x_holder(sigma)
            )
        for delta in z_order[:-1]:
            for slot in (2 * delta, 2 * delta + 1):
                mirrored[half, slot] = backward(slot)
            block = pl.ds(2 * delta, 2)
            push(
                mirrored.at[half, block], to_z.at[half, block], ("bz" + turn, half), z_holder(delta)
            )

    inner = pl.ds(2, z_slots - 2)

    def summed(from_z, from_x, target, half):
        def strip(index, carry):
            here = pl.ds(pl.multiple_of(index * 8, 8), 8)
            there = pl.ds(pl.multiple_of(half * part + index * 8, 8), 8)
            totals = [diag[t, there, :] for t in range(each)]
            slots = [(from_z, slot, slot // 2, slot % 2) for slot in range(2, z_slots)]
            slots += [(from_x, slot, chips + slot // 2, slot % 2) for slot in range(x_slots)]
            for source, slot, peer, place in slots:
                value = source[half, slot, here, :]
                asked = lax.shift_right_logical(wanted[peer, place : place + 1, :], 16) & 255
                for t in range(each):
                    hit = jnp.broadcast_to(asked == t, (8, 128))
                    hit = jnp.concatenate([hit] * (size // 128), axis=1)
                    totals[t] = totals[t] + jnp.where(hit, value, 0.0)
            for t in range(each):
                target[t, there, :] = totals[t]
            return carry

        lax.fori_loop(0, part // 8, strip, 0)

    def all_rows(buffer, slot):
        return jnp.concatenate([buffer[half, slot] for half in range(halves)], axis=0)

    def rows_held(buffers, slot):
        return jnp.concatenate([buffer[slot] for buffer in buffers], axis=0)

    for half in range(halves):
        answer(base, rz1, rx1, sz1, sx1, "1", half)
    for slot in range(z_slots):
        weight_sz[slot] = weight[z_asked(slot)]
    for slot in range(x_slots):
        weight_sx[slot] = weight[x_asked(slot)]
    for delta in range(chips):
        block = pl.ds(2 * delta, 2)
        push(weight_sz.at[block], weight_rz.at[block], "weight_z", z_reader(delta))
    for sigma in range(1, reps):
        block = pl.ds(2 * (sigma - 1), 2)
        push(weight_sx.at[block], weight_rx.at[block], "weight_x", x_reader(sigma))
    own_mid = jnp.zeros((2 * count, 3 * count), F32)
    for t in range(each):
        own_mid = own_mid + dot_t(stacked(diag[t]), scaled(base[t], weight[t]))
    other_load.wait()
    for half in range(halves):
        landed(rz1.at[half], ("z1", half))
        landed(rx1[half], ("x1", half))
        if half == 0:
            landed(low_b, "low_b")
            low_piece[1] = total(low_b)
            spread(low_piece.at[1], low_c, "low_c", "row")
        returned(
            lambda slot: dot_t(rz1[half, slot].astype(BF16), tile_of(slot)),
            lambda slot: dot(rx1[half][x_of(slot)].astype(BF16), tile_of(slot)),
            prod_i1,
            prod_j1,
            tx1,
            bz1,
            bx1,
            "1",
            half,
        )
    landed(low_c, "low_c")
    joined(low_c, low)
    landed(weight_rz, "weight_z")
    landed(weight_rx, "weight_x")

    def used(slot):
        return z_code(slot) >= 16777216

    own_form = own_mid[:, :count]
    both_form = jnp.zeros((2 * count, count), F32)
    scaled_form = own_mid[:, count : 2 * count] + own_mid[:, 2 * count :]
    for slot in range(z_slots):
        there = x_of(slot)
        product = dot_t(
            stacked(all_rows(prod_i1, slot)), scaled(rows_held(rx1, there), weight_rx[there])
        )
        product = jnp.where(used(slot), product, 0.0)
        if slot < 2:
            own_form = own_form + product[:, :count]
        else:
            both_form = both_form + product[:, :count]
        scaled_form = scaled_form + product[:, count : 2 * count] + product[:, 2 * count :]
        if slot >= 2:
            product = dot_t(
                stacked(all_rows(prod_j1, slot)),
                stacked(all_rows(rz1, slot) * weight_rz[slot]),
            )
            product = jnp.where(used(slot), product, 0.0)
            scaled_form = scaled_form + product[:, :count] + product[:, count:]
    both_form = folded(both_form + 0.5 * own_form)
    scaled_form = folded(scaled_form)
    quarter = jnp.concatenate([both_form, scaled_form], axis=1) * scale
    mid_m[...] = jnp.concatenate([quarter[: count // 2], quarter[count // 2 :]], axis=1)
    spread(mid_m, mid_a, "mid_a", "row")

    for half in range(halves):
        landed(bz1.at[half, inner], ("bz1", half))
        landed(bx1.at[half], ("bx1", half))
        summed(bz1, bx1, applied, half)
        if half == halves - 1:
            landed(mid_a, "mid_a")
            mid_n[...] = total(mid_a)
            spread(mid_n, mid_b, "mid_b", "rep")
        answer(applied, rz2, rx2, sz2, sx2, "2", half)
    landed(mid_b, "mid_b")
    quarter = total(mid_b)
    quarter = jnp.concatenate([quarter[:, : 2 * count], quarter[:, 2 * count :]], axis=0)
    basis_applied = quarter[:, :count] + quarter[:, :count].T
    scaled_applied = quarter[:, count:]
    basis_gram = jnp.concatenate([low[:, :count], low[:, 2 * count : 3 * count]], axis=0)
    scaled_gram = jnp.concatenate([low[:, count : 2 * count], low[:, 3 * count :]], axis=0)
    row_of = lax.broadcasted_iota(jnp.int32, (count, count), 0)
    col_of = lax.broadcasted_iota(jnp.int32, (count, count), 1)
    ritz = jnp.sum(jnp.where(row_of == col_of, basis_applied, 0.0), axis=1, keepdims=True)
    correlation = basis_applied - ritz * basis_gram
    mixed = correlation + jnp.where(row_of == col_of, ritz, 0.0)
    coefficients = exact(mixed, scaled_gram) - scaled_applied

    for half in range(halves):
        here = rows_of(half)
        both = stacked(jnp.concatenate([mixed[here], coefficients[here]], axis=0))

        def rebuilt(block, image, scaling):
            parts = folded(dot(both, block.astype(BF16)))
            remainder = parts[:part] - image
            return scaling * remainder - parts[part:], remainder

        def forward(slot):
            value, unused = rebuilt(all_rows(rz1, slot), rz2[half, slot], weight_rz[slot])
            return folded(dot_t(stacked(value), tile_of(slot)))

        def backward(slot):
            there = x_of(slot)
            value, unused = rebuilt(rows_held(rx1, there), rx2[half][there], weight_rx[there])
            return folded(dot(stacked(value), tile_of(slot)))

        landed(rz2.at[half], ("z2", half))
        landed(rx2[half], ("x2", half))
        returned(forward, backward, prod_i2, prod_j2, tx2, bz2, bx2, "2", half)
        for t in range(each):
            value, remainder = rebuilt(base[t], applied[t, here, :], weight[t])
            seed[t, here, :] = value
            right[t, here, :] = remainder
            diag[t, here, :] = folded(dot_t(stacked(value), tiles[t]))

    for half in range(halves):
        here = rows_of(half)
        landed(bz2.at[half, inner], ("bz2", half))
        landed(bx2.at[half], ("bx2", half))
        summed(bz2, bx2, updated, half)
        for t in range(each):
            value = seed[t, here, :]
            updated[t, here, :] = value + weight[t] * (
                right[t, here, :] - (updated[t, here, :] - ritz[here] * value)
            )
        if half == halves - 1:
            second = jnp.zeros((2 * count, 5 * count), F32)
            for t in range(each):
                parts = split(updated[t])
                second = second + dot_t(
                    jnp.concatenate(parts, axis=0),
                    jnp.concatenate([*parts, base[t].astype(BF16), *split(applied[t])], axis=0),
                )
            second = folded(second) * scale
            second = jnp.concatenate(
                [
                    second[:, :count] + second[:, count : 2 * count],
                    second[:, 2 * count : 3 * count],
                    second[:, 3 * count : 4 * count] + second[:, 4 * count :],
                    jnp.zeros((count, count), F32),
                ],
                axis=1,
            )
            cut(second, new_m)
            scatter(new_m, new_a, "new_a")
        answer(updated, rz3, rx3, sz3, sx3, "3", half)
    form = jnp.zeros((2 * count, 2 * count), F32)
    for t in range(each):
        value = stacked(updated[t])
        form = form + dot_t(value, stacked(folded(dot_t(value, tiles[t]))))
    form = 0.5 * form
    landed(new_a, "new_a")
    new_piece[0] = total(new_a)
    spread(new_piece.at[0], new_b, "new_b", "rep")
    for half in range(halves):
        landed(rz3.at[half], ("z3", half))
        landed(rx3[half], ("x3", half))
        if half == halves - 1:
            landed(new_b, "new_b")
            new_piece[1] = total(new_b)
            spread(new_piece.at[1], new_c, "new_c", "row")
        for slot in range(z_slots):
            prod_i2[half, slot] = folded(dot_t(stacked(rz3[half, slot]), tile_of(slot)))
    for slot in range(z_slots):
        product = dot_t(stacked(rows_held(rx3, x_of(slot))), stacked(all_rows(prod_i2, slot)))
        form = form + jnp.where(used(slot), 0.5 if slot < 2 else 1.0, 0.0) * product
    form = folded(form)
    form = (form[:, :count] + form[:, count:]) * scale
    lines = count // 4
    end_m[...] = jnp.concatenate([form[i * lines : (i + 1) * lines] for i in range(4)], axis=1)
    spread(end_m, end_a, "end_a", "row")

    landed(new_c, "new_c")
    joined(new_c, new)
    new_gram = new[:, :count]
    overlap = new[:, count : 2 * count]
    new_applied = new[:, 2 * count : 3 * count]
    identity = (row_of == col_of).astype(F32)
    correction_gram = new_gram - exact_t(exact(overlap, 2.0 * identity - basis_gram), overlap)
    work = eliminated(jnp.concatenate([correction_gram, identity], axis=1), 0, count // 2)
    landed(end_a, "end_a")
    end_n[...] = total(end_a)
    spread(end_n, end_b, "end_b", "rep")
    inverse = eliminated(work, count // 2, count)[:, count:]
    turned = exact(overlap, basis_applied)
    cross = new_applied - turned
    known = exact_t(new_applied, overlap)
    known = exact_t(turned, overlap) - known - exact_t(overlap, new_applied)
    projected[:count, :count] = basis_applied
    projected[count:, :count] = exact(inverse, cross)
    projected[:count, count:] = exact_t(cross.T, inverse)
    for t in range(each):
        value = updated[t] - folded(dot(stacked(overlap), base[t].astype(BF16)))
        directions[:, t * size : (t + 1) * size] = exact(inverse, value)
    landed(end_b, "end_b")
    form = total(end_b)
    form = jnp.concatenate([form[:, i * count : (i + 1) * count] for i in range(4)], axis=0)
    middle = form + form.T + known
    projected[count:, count:] = exact_t(exact(inverse, middle), inverse)

    gone(request, "request")
    gone(weight_sz, "weight_z")
    gone(weight_sx, "weight_x")
    for half in range(halves):
        for turn, from_z, from_x in (("1", sz1, sx1), ("2", sz2, sx2), ("3", sz3, sx3)):
            gone(from_z.at[half], ("z" + turn, half))
            gone(from_x.at[half], ("x" + turn, half))
        for turn, from_z, from_x in (("1", prod_j1, tx1), ("2", prod_j2, tx2)):
            gone(from_z.at[half, inner], ("bz" + turn, half))
            gone(from_x.at[half], ("bx" + turn, half))
    other_rows = pl.ds(0, rows - 1)
    other_reps = pl.ds(0, reps - 1)
    for key, buffer in (
        ("low_a", low_a.at[other_rows]),
        ("low_b", low_b.at[other_reps]),
        ("low_c", low_c.at[other_rows]),
        ("mid_a", mid_a.at[other_rows]),
        ("mid_b", mid_b.at[other_reps]),
        ("new_a", new_a.at[other_rows]),
        ("new_b", new_b.at[other_reps]),
        ("new_c", new_c.at[other_rows]),
        ("end_a", end_a.at[other_rows]),
        ("end_b", end_b.at[other_reps]),
    ):
        gone(buffer, key)


def publish(directions, projected, directions_out, projected_out):
    directions_out[...] = directions[...]
    projected_out[...] = projected[...]


def shards(basis, precond, tiles, tile_rows, tile_cols):
    count, shard = basis.shape
    size = tiles.shape[1]
    each = shard // size
    rows = lax.axis_size("row")
    reps = lax.axis_size("rep")
    chips = rows // 2
    halves = 2
    asked = (chips + reps - 1, 2, 128)
    z_slots = 2 * chips
    x_slots = 2 * (reps - 1)

    def held(*shape):
        return pltpu.VMEM(shape, F32)

    z_block = held(halves, z_slots, count // halves, size)
    x_block = held(halves, x_slots, count // halves, size)
    x_half = held(x_slots, count // halves, size)
    own = held(each, count, size)
    wide = 4 * count
    lines = count // rows
    scratch = [
        pltpu.VMEM(asked, jnp.int32),
        pltpu.SMEM(asked, jnp.int32),
        pltpu.VMEM(basis.shape, BF16),
        held(1, shard),
        pltpu.VMEM(tiles.shape, BF16),
        pltpu.VMEM(asked, jnp.int32),
        pltpu.SMEM(asked, jnp.int32),
        own,
        held(each, 1, size),
        held(z_slots, 1, size),
        held(x_slots, 1, size),
        held(z_slots, 1, size),
        held(x_slots, 1, size),
        *([z_block, x_block, z_block, *([x_half] * halves)] * 3),
        z_block,
        z_block,
        z_block,
        z_block,
        x_block,
        x_block,
        z_block,
        x_block,
        z_block,
        x_block,
        *([own] * 5),
        held(rows, lines // 2, wide),
        held(rows, lines // 2, wide),
        held(reps, lines // 2, wide),
        held(rows, lines // 2, wide),
        held(2, lines // 2, wide),
        held(count // 2, wide),
        held(count // 2, wide),
        held(rows, count // 2, wide),
        held(count // 2, wide),
        held(reps, count // 2, wide),
        held(rows, lines, wide),
        held(rows, lines, wide),
        held(reps, lines, wide),
        held(rows, lines, wide),
        held(2, lines, wide),
        held(count, wide),
        held(count // 4, wide),
        held(rows, count // 4, wide),
        held(count // 4, wide),
        held(reps, count // 4, wide),
        pltpu.SemaphoreType.DMA((len(KEYS),)),
        pltpu.SemaphoreType.DMA((len(KEYS),)),
        pltpu.SemaphoreType.DMA((6,)),
    ]
    vmem = pl.BlockSpec(memory_space=pltpu.VMEM)
    far_away = pl.BlockSpec(memory_space=pl.ANY)
    found = pl.pallas_call(
        functools.partial(kernel, rows, reps, halves, 1.0 / (shard * rows * reps)),
        name="davidson_step",
        out_shape=(
            jax.ShapeDtypeStruct((count, shard), F32),
            jax.ShapeDtypeStruct((2 * count, 2 * count), F32),
        ),
        in_specs=[vmem, vmem, far_away, far_away, far_away],
        out_specs=(vmem, vmem),
        scratch_shapes=scratch,
        compiler_params=pltpu.CompilerParams(
            collective_id=0, has_side_effects=True, vmem_limit_bytes=60 * 1024 * 1024
        ),
    )(
        tile_rows.reshape(1, tile_rows.shape[0]),
        tile_cols.reshape(1, tile_cols.shape[0]),
        basis,
        precond.reshape(1, shard),
        tiles,
    )
    return pl.pallas_call(
        publish,
        name="publish",
        out_shape=tuple(jax.ShapeDtypeStruct(a.shape, a.dtype) for a in found),
        in_specs=[vmem, vmem],
        out_specs=(vmem, vmem),
    )(*found)


def solution(mesh):
    both = ("row", "rep")
    placed = (P(None, both), P(both), P(both, None, None), P(both), P(both))
    return jax.shard_map(
        shards, mesh=mesh, in_specs=placed, out_specs=(P(None, both), P()), check_vma=False
    )
```
